32 devices in a mesh: parts: 2 (over x), src: 8 (over z, y), tile: 2 (over core).
Axes of the slice: x: 2, y: 2, z: 4, core: 2. Of those that a mesh axis runs over, the one named last changes fastest.
Arguments:
- mask_values: bfloat16 [2048, 512], P(('parts', 'tile')), parts along dimension 0, may hold values from -1 to 1
- target_image: float32 [2048, 512], P(('parts', 'tile')), parts along dimension 0, may hold values from 0 to 1.5
- jones_pupil: float32 [2, 3, 2, 128, 128], replicated, may hold values from -1.7 to 1.7
- polar_states: float32 [4, 2, 2], replicated, may hold values from -3 to 3
- source_weights: float32 [64], P(('parts', 'src')), parts along dimension 0, may hold values from 0.25 to 4
- pupil_offsets: int32 [64, 2], P(('parts', 'src')), parts along dimension 0, may hold values from 0 to 64
- polar_ids: int32 [64], P(('parts', 'src')), parts along dimension 0, may hold values from 0 to 3
Outputs:
- intensity: float32 [4, 512, 512], P(('parts', 'tile'), 'src'), parts along dimension 0
- mask_grad: float32 [4, 512, 512], P(('parts', 'tile'), 'src'), parts along dimension 0
- source_grad: float32 [64], P(('parts', 'src')), parts along dimension 0
The draws below stay inside these ranges and needn't reach their ends.
There are 2 independent parts, one for each index of `parts`. The reference program is written for one: setup_inputs(seed, part) draws one part's arguments, and reference() takes and returns one part's arrays. A program takes and returns all parts, laid end to end along the dimension named above; an argument that names none is the same for every part. Nothing has to cross between parts.
All inputs are finite; a program needn't handle non-finite values.
Results may differ from the reference program's by a relative error of at most 0.018.
Values may be sent and summed in bfloat16 or wider, within the bound.
No kernel may reach another device: no remote copies, remote signals or barrier semaphores. Data moves between devices by JAX's collectives and lax.ppermute only.
A program may use at most 64 MiB of HBM per device.

```python
import math
import jax
import jax.numpy as jnp
from jax import lax

TH = 512
TW = 512
AMB = 64
K = 64
NPOL = 4
KP = 128
NS = 32
ROWS = 1024
N_TILE = 2


def draw_jones_pupil(key, part):
    key_angle, key_rough = jax.random.split(jax.random.fold_in(key, 11))
    angle = jax.random.uniform(key_angle, (3, 2), jnp.float32, -math.pi, math.pi)
    magnitude = 0.7
    rough = jnp.clip(0.3 * jax.random.normal(key_rough, (2, 3, 2, KP, KP), jnp.float32), -1.0, 1.0)
    common = magnitude * jnp.stack([jnp.cos(angle), jnp.sin(angle)], 0)
    return common[:, :, :, None, None] + rough


def draw_target_image(key, part):
    keys = jax.random.split(jax.random.fold_in(key, 23), 4)
    row_cycles = (jax.random.randint(keys[0], (), 1, 3) * max(1, TH // 64)).astype(jnp.float32)
    col_cycles = (jax.random.randint(keys[1], (), 1, 3) * max(1, TW // 64)).astype(jnp.float32)
    phase = jax.random.uniform(keys[2], (), jnp.float32, -math.pi, math.pi)
    row_pos = jnp.arange(ROWS, dtype=jnp.float32)
    col_pos = jnp.arange(TW, dtype=jnp.float32)
    angle = 2.0 * math.pi * (row_cycles * row_pos[:, None] / TH + col_cycles * col_pos[None, :] / TW) + phase
    smooth = jnp.cos(angle)
    amplitude = 0.45
    rough = jax.random.uniform(keys[3], (ROWS, TW), jnp.float32, -0.25, 0.25)
    return 0.75 + amplitude * smooth + rough


def set_ends(values, stream_key, smallest, largest):
    longest = values.shape.index(max(values.shape))
    spots = []
    for shift in (0, 1):
        where = [jax.random.randint(jax.random.fold_in(stream_key, axis), (), 0, length) for axis, length in enumerate(values.shape)]
        where[longest] = (where[longest] + shift) % values.shape[longest]
        spots.append(tuple(where))
    return values.at[spots[0]].set(smallest).at[spots[1]].set(largest)


def block_levels(own_key, shape, cuts, least, largest):
    def one(dim, blocks):
        steps = jax.random.uniform(jax.random.fold_in(jax.random.fold_in(own_key, 6), dim), (blocks,), jnp.float32, least / len(cuts), largest / len(cuts))
        return jnp.repeat(jnp.exp(steps), shape[dim] // blocks).reshape((-1,) + (1,) * (len(shape) - dim - 1))

    level = one(*cuts[0])
    for cut in cuts[1:]:
        level = level * one(*cut)
    return level


def normal_values(key, shape, spread, reach, held_as=jnp.bfloat16):
    return jnp.clip(spread * jax.random.normal(key, shape, jnp.float32), -reach, reach).astype(held_as)


def setup_inputs(seed: int = 0, part: int = 0) -> dict:
    arg_keys = jax.random.split(jax.random.key(seed), 8)
    part_splits = jax.random.split(jax.random.fold_in(arg_keys[7], part), 8)
    mask_values = jnp.clip(jax.random.uniform(part_splits[0], (ROWS, TW), jnp.float32, -1.0, 1.0) * block_levels(part_splits[0], (ROWS, TW), ((0, 2),), -0.4, 0.0), -1.0, 1.0).astype(jnp.bfloat16)
    target_image = draw_target_image(jax.random.fold_in(jax.random.fold_in(arg_keys[7], part), 71), part)
    jones_pupil = draw_jones_pupil(jax.random.fold_in(arg_keys[7], 71), part)
    polar_states = normal_values(arg_keys[3], (NPOL, 2, 2), 0.7, 3.0, jnp.float32)
    source_weights = jnp.clip(jnp.exp(math.log(4.0) - 2.7725887 * jax.random.uniform(part_splits[4], (NS,), jnp.float32) ** block_levels(part_splits[4], (NS,), ((0, 8),), -0.2, 0.2)), 0.25, 4.0)
    pupil_offsets = set_ends(jax.random.randint(part_splits[5], (NS, 2), 0, K + 1), jax.random.fold_in(part_splits[5], 1), 0, K).astype(jnp.int32)
    polar_ids = set_ends(jax.random.randint(part_splits[6], (NS,), 0, NPOL), jax.random.fold_in(part_splits[6], 1), 0, NPOL - 1).astype(jnp.int32)
    return dict(mask_values=mask_values, target_image=target_image, jones_pupil=jones_pupil, polar_states=polar_states, source_weights=source_weights, pupil_offsets=pupil_offsets, polar_ids=polar_ids)


TWO_PI = 2.0 * math.pi
GRAD_SCALE = 32.0

def tables():
    window = TH + 2 * AMB
    orders = jnp.arange(K, dtype=jnp.int32) - K // 2
    columns = jnp.arange(TW, dtype=jnp.int32)
    win_rows = jnp.arange(window, dtype=jnp.int32)
    core_rows = jnp.arange(TH, dtype=jnp.int32) + AMB
    col_angle = TWO_PI * jnp.mod(columns[:, None] * orders[None, :], TW).astype(jnp.float32) / TW
    row_angle = TWO_PI * jnp.mod(orders[:, None] * win_rows[None, :], window).astype(jnp.float32) / window
    core_angle = TWO_PI * jnp.mod(core_rows[:, None] * orders[None, :], window).astype(jnp.float32) / window
    col_fwd = jnp.concatenate([jnp.cos(col_angle), -jnp.sin(col_angle)], 1).astype(jnp.bfloat16)
    row_fwd = jnp.concatenate([jnp.cos(row_angle), jnp.sin(row_angle)], 0).astype(jnp.bfloat16)
    upper_rows = jnp.concatenate([jnp.cos(core_angle), -jnp.sin(core_angle)], 1)
    lower_rows = jnp.concatenate([jnp.sin(core_angle), jnp.cos(core_angle)], 1)
    row_inv = jnp.concatenate([upper_rows, lower_rows], 0).astype(jnp.bfloat16)
    cos_cols = jnp.cos(col_angle).T
    sin_cols = jnp.sin(col_angle).T
    col_inv = jnp.concatenate([jnp.concatenate([cos_cols, sin_cols], 1), jnp.concatenate([-sin_cols, cos_cols], 1)], 0).astype(jnp.bfloat16)
    return (col_fwd, row_fwd, row_inv, col_inv)

def spectrum(extended, col_fwd, row_fwd):
    partial_dft = jnp.dot(extended, col_fwd, preferred_element_type=jnp.float32).astype(jnp.bfloat16)
    product = jnp.dot(row_fwd, partial_dft, preferred_element_type=jnp.float32)
    norm_scale = 1.0 / math.sqrt((TH + 2 * AMB) * TW)
    spectrum_re = norm_scale * (product[:K, :K] + product[K:, K:])
    spectrum_im = norm_scale * (product[:K, K:] - product[K:, :K])
    return (spectrum_re, spectrum_im)

def pupil_of(jones_pupil, polar_states, offset, state_id):
    one_hot = (jnp.arange(NPOL, dtype=jnp.int32) == state_id.astype(jnp.int32)).astype(jnp.float32)
    jones_vec = lax.optimization_barrier(jnp.sum(one_hot[:, None, None] * polar_states, 0))
    zero_index = jnp.zeros((), jnp.int32)
    window = lax.dynamic_slice(jones_pupil, (zero_index, zero_index, zero_index, offset[0].astype(jnp.int32), offset[1].astype(jnp.int32)), (2, 3, 2, K, K))
    vec_re = jones_vec[0][None, :, None, None]
    vec_im = jones_vec[1][None, :, None, None]
    pupil_re = lax.optimization_barrier(jnp.sum(window[0] * vec_re - window[1] * vec_im, 1))
    pupil_im = lax.optimization_barrier(jnp.sum(window[0] * vec_im + window[1] * vec_re, 1))
    return (pupil_re, pupil_im)

def masked_stack(pupil_re, pupil_im, spectrum_re, spectrum_im):
    masked_re = pupil_re * spectrum_re - pupil_im * spectrum_im
    masked_im = pupil_re * spectrum_im + pupil_im * spectrum_re
    return jnp.concatenate([masked_re, masked_im], 1).astype(jnp.bfloat16)

def row_field_of(stacked, row_inv):
    rows_out = jnp.einsum('ak,ckl->cal', row_inv.astype(jnp.float32), stacked.astype(jnp.float32))
    return jnp.concatenate([rows_out[:, :TH], rows_out[:, TH:]], 2).astype(jnp.bfloat16)

def field_of(row_field, col_inv):
    return jnp.einsum('cpk,kq->cpq', row_field.astype(jnp.float32), col_inv.astype(jnp.float32)) / K

def intensity_of(field):
    return lax.optimization_barrier(jnp.sum(field[..., :TW] * field[..., :TW] + field[..., TW:] * field[..., TW:], 0))

def adjoint_terms(field, residual, weight, pupil_re, pupil_im, row_inv, col_inv, source_total):
    coefficient = 2.0 * weight / (source_total * K)
    doubled = jnp.concatenate([residual, residual], 1)
    field_grad = (coefficient * doubled[None] * field).astype(jnp.bfloat16)
    row_grad = jnp.einsum('cpq,kq->cpk', field_grad.astype(jnp.float32), col_inv.astype(jnp.float32)).astype(jnp.bfloat16)
    stacked = jnp.concatenate([row_grad[..., :K], row_grad[..., K:]], 1)
    masked_grad = jnp.einsum('ak,cal->ckl', row_inv.astype(jnp.float32), stacked.astype(jnp.float32))
    grad_re = masked_grad[:, :K]
    grad_im = masked_grad[:, K:]
    spec_re = lax.optimization_barrier(jnp.sum(pupil_re * grad_re + pupil_im * grad_im, 0))
    spec_im = lax.optimization_barrier(jnp.sum(pupil_re * grad_im - pupil_im * grad_re, 0))
    return (spec_re, spec_im)

def window_grad(grad_re, grad_im, row_fwd, col_fwd):
    norm_scale = 1.0 / math.sqrt((TH + 2 * AMB) * TW)
    top_rows = jnp.concatenate([grad_re, grad_im], 1)
    bottom_rows = jnp.concatenate([-grad_im, grad_re], 1)
    grad_prod = norm_scale * jnp.concatenate([top_rows, bottom_rows], 0)
    grad_partial = jnp.dot(row_fwd.astype(jnp.float32).T, grad_prod, precision=lax.Precision.HIGHEST)
    return jnp.dot(grad_partial, col_fwd.astype(jnp.float32).T, precision=lax.Precision.HIGHEST)

def reference(mask_values, target_image, jones_pupil, polar_states, source_weights, pupil_offsets, polar_ids):
    col_fwd, row_fwd, row_inv, col_inv = tables()
    window = TH + 2 * AMB
    tile_count = N_TILE
    source_total = source_weights.shape[0]
    padded = jnp.pad(mask_values, ((AMB, AMB), (0, 0)))
    spectra = [spectrum(padded[tile_index * TH:tile_index * TH + window], col_fwd, row_fwd) for tile_index in range(tile_count)]
    targets = target_image.reshape(tile_count, TH, TW)

    def forward(running, item):
        weight, offset, state_id = item
        pupil_re, pupil_im = pupil_of(jones_pupil, polar_states, offset, state_id)
        updates = []
        for tile_index in range(tile_count):
            stacked = masked_stack(pupil_re, pupil_im, spectra[tile_index][0], spectra[tile_index][1])
            field = field_of(row_field_of(stacked, row_inv), col_inv)
            updates.append(weight / source_total * intensity_of(field))
        return (running + jnp.stack(updates), jnp.zeros((), jnp.float32))
    intensity, unused = lax.scan(forward, jnp.zeros((tile_count, TH, TW), jnp.float32), (source_weights, pupil_offsets, polar_ids))
    residual = intensity - targets

    def backward(running, item):
        weight, offset, state_id = item
        pupil_re, pupil_im = pupil_of(jones_pupil, polar_states, offset, state_id)
        new_re = []
        new_im = []
        terms = []
        for tile_index in range(tile_count):
            stacked = masked_stack(pupil_re, pupil_im, spectra[tile_index][0], spectra[tile_index][1])
            field = field_of(row_field_of(stacked, row_inv), col_inv)
            terms.append(jnp.sum(residual[tile_index] * intensity_of(field)))
            spec_re, spec_im = adjoint_terms(field, residual[tile_index], weight, pupil_re, pupil_im, row_inv, col_inv, source_total)
            new_re.append(running[0][tile_index] + spec_re)
            new_im.append(running[1][tile_index] + spec_im)
        return ((jnp.stack(new_re), jnp.stack(new_im)), jnp.sum(jnp.stack(terms)))
    empty = jnp.zeros((tile_count, K, K), jnp.float32)
    (grad_re, grad_im), weight_terms = lax.scan(backward, (empty, empty), (source_weights, pupil_offsets, polar_ids))
    source_grad = weight_terms / (tile_count * TH * TW)
    grad_rows = jnp.zeros((tile_count * TH + 2 * AMB, TW), jnp.float32)
    for tile_index in range(tile_count):
        grad_rows = grad_rows.at[tile_index * TH:tile_index * TH + window].add(window_grad(grad_re[tile_index], grad_im[tile_index], row_fwd, col_fwd))
    mask_grad = GRAD_SCALE * grad_rows[AMB:AMB + tile_count * TH].reshape(tile_count, TH, TW)
    return (intensity, mask_grad, source_grad)
```

```python
import math

import jax
import jax.numpy as jnp
import numpy as np
from jax import lax
from jax.experimental import pallas as pl
from jax.experimental.pallas import tpu as pltpu
from jax.sharding import PartitionSpec as P

AMB = 64
K = 64
GRID = 2 * K
GRAD_SCALE = 32.0
F32 = jnp.float32
BF16 = jnp.bfloat16


def flip(value, axis, mask):
    pairs = [(i, i ^ mask) for i in range(lax.axis_size(axis))]
    return lax.ppermute(value, axis, pairs)


def narrow(table):
    return np.asarray(table, np.float32).astype(jnp.bfloat16)


def split(table):
    high = narrow(table)
    return high, narrow(np.asarray(table, np.float64) - high.astype(np.float64))


def kernel_of_orders(gap):
    orders = np.arange(1, K)
    return (1.0 + 2.0 * np.cos(gap[..., None] * orders).sum(-1)) / GRID


def make_tables(tile_h, tile_w, tiles):
    window = tile_h + 2 * AMB
    two_pi = 2.0 * math.pi
    orders = np.arange(K) - K // 2
    cols = np.arange(tile_w)
    rows = np.arange(window)
    points = np.arange(GRID)
    col = two_pi * np.mod(cols[:, None] * orders[None], tile_w) / tile_w
    row = two_pi * np.mod(orders[:, None] * rows[None], window) / window
    grid = two_pi * np.mod(orders[:, None] * points[None], GRID) / GRID
    cos, sin = np.cos(grid), np.sin(grid)
    col_fwd = np.concatenate([np.cos(col), -np.sin(col)], 1)
    row_fwd = np.concatenate([np.cos(row), np.sin(row)], 0)
    cols_out = np.block([[cos, sin], [-cos, -sin], [-sin, cos], [-sin, cos]])
    rows_out = np.block([[cos.T, -sin.T], [sin.T, cos.T]])
    cols_back = np.block(
        [[cos.T, -sin.T, -sin.T, cos.T], [sin.T, cos.T, cos.T, sin.T]]
    )
    core = np.arange(tile_h) + AMB
    lift_rows = kernel_of_orders(
        two_pi * (core[:, None] / window - points[None] / GRID)
    )
    lift_cols = kernel_of_orders(
        two_pi * (points[:, None] / GRID - cols[None] / tile_w)
    )
    gram = (tile_w / GRID) * lift_rows.T @ lift_rows
    halo = np.stack([row_fwd[:, tile_h + AMB :], row_fwd[:, :AMB]])
    own_rows = row_fwd[:, AMB : AMB + tile_h].T
    other = np.zeros((tiles, tile_h, 2 * K))
    other[0, tile_h - AMB :] = row_fwd[:, :AMB].T
    other[1, :AMB] = row_fwd[:, tile_h + AMB :].T
    back_rows = np.concatenate([np.broadcast_to(own_rows, other.shape), other], 2)
    return dict(
        col_fwd=narrow(col_fwd),
        col_fwd_t=narrow(col_fwd.T),
        row_core=narrow(row_fwd[:, AMB : AMB + tile_h]),
        row_halo=narrow(halo),
        cols_out=narrow(cols_out),
        rows_out=narrow(rows_out),
        rows_back=narrow(rows_out.T),
        cols_back=narrow(cols_back),
        lift_rows=narrow(lift_rows),
        lift_rows_t=narrow(lift_rows.T),
        lift_cols=narrow(lift_cols),
        lift_cols_t=narrow(lift_cols.T),
        gram=np.stack(split(gram)),
        back_rows=narrow(back_rows),
    )


def dot(a, b):
    return jnp.dot(a, b, preferred_element_type=F32)


def halves(value):
    high = value.astype(BF16)
    return high, (value - high.astype(F32)).astype(BF16)


def dot_wide(table, value):
    high, low = halves(value)
    return dot(table, high) + dot(table, low)


def wide_dot(value, table):
    high, low = halves(value)
    return dot(high, table) + dot(low, table)


def lanes(shape):
    return lax.broadcasted_iota(jnp.int32, shape, 1)


def source_kernel(
    weight, offset, state, polar, place,
    mask, halo, target, jones,
    col_fwd, row_core, row_halo, cols_out, rows_out, rows_back, cols_back,
    lift_rows_t, lift_cols_t, gram,
    image_out, grad_out,
    tables, pupils, stack, fields, powers, image, held, wide,
):
    groups, each = weight.shape
    count = 3 * each
    norm = 1.0 / math.sqrt((mask.shape[0] + 2 * AMB) * mask.shape[1])
    left = lanes((K, GRID)) < K

    for pol in range(polar.shape[0] // 4):
        ar, br, ai, bi = (polar[4 * pol + n] for n in range(4))
        for j in range(3):
            real = jones[2 * j] * ar - jones[6 + 2 * j] * ai
            real += jones[2 * j + 1] * br - jones[6 + 2 * j + 1] * bi
            imag = jones[2 * j] * ai + jones[6 + 2 * j] * ar
            imag += jones[2 * j + 1] * bi + jones[6 + 2 * j + 1] * br
            tables[2 * (3 * pol + j)] = real
            tables[2 * (3 * pol + j) + 1] = pltpu.roll(imag, K, 1)

    part = dot(mask[...], col_fwd[...]).astype(BF16)
    edge = dot(halo[...], col_fwd[...]).astype(BF16)
    product = dot(row_core[...], part) + dot(row_halo[place[0]], edge)
    turned = pltpu.roll(product[K:], K, 1)
    first = norm * (product[:K] + jnp.where(left, turned, -turned))
    second = pltpu.roll(first, K, 1)

    seen = dot(lift_rows_t[...], target[...].astype(BF16)).astype(BF16)
    wanted = dot(seen, lift_cols_t[...])

    image[...] = jnp.zeros_like(image)

    def forward(group, carry):
        for s in range(each):
            up = offset[group, 2 * s]
            side = offset[group, 2 * s + 1]
            pol = state[group, s]
            inside = (lanes((K, GRID)) >= side) & (lanes((K, GRID)) < side + K)
            turn = jnp.where(side == 0, 0, GRID - side)
            for j in range(3):
                real = tables[2 * (3 * pol + j), pl.ds(up, K), :]
                imag = tables[2 * (3 * pol + j) + 1, pl.ds(up, K), :]
                pupil = pltpu.roll(jnp.where(inside, real, imag), turn, 1)
                f = 3 * s + j
                pupils[group, f] = pupil
                stack[f * K : (f + 1) * K, :GRID] = (pupil * first).astype(BF16)
                stack[f * K : (f + 1) * K, GRID:] = (pupil * second).astype(BF16)
        across = dot(stack[...], cols_out[...]).astype(BF16)
        for f in range(count):
            rows = across[f * K : (f + 1) * K]
            held[:K, f * GRID : (f + 1) * GRID] = rows[:, :GRID]
            held[K:, f * GRID : (f + 1) * GRID] = rows[:, GRID:]
        for s in range(each):
            power = None
            for j in range(3):
                f = 3 * s + j
                field = dot(rows_out[...], held[:, f * GRID : (f + 1) * GRID])
                fields[group, :, f * GRID : (f + 1) * GRID] = field.astype(BF16)
                square = field[:GRID] * field[:GRID] + field[GRID:] * field[GRID:]
                power = square if power is None else power + square
            powers[group, s] = power
            image[...] += weight[group, s] * power
        return carry

    lax.fori_loop(0, groups, forward, 0)
    total = image[...] * (1.0 / (groups * each * K * K))
    image_out[...] = total

    high, low = halves(total)
    rho = dot(gram[0], high) + dot(gram[0], low) + dot(gram[1], high) - wanted
    double = jnp.concatenate([rho, rho], 0).astype(BF16)

    grad_out[...] = jnp.zeros_like(grad_out)
    wide[...] = jnp.zeros_like(wide)

    def backward(group, carry):
        for f in range(count):
            rated = fields[group, :, f * GRID : (f + 1) * GRID] * double
            down = dot(rows_back[...], rated).astype(BF16)
            stack[f * K : (f + 1) * K, :GRID] = down[:K]
            stack[f * K : (f + 1) * K, GRID:] = down[K:]
        back = dot(stack[...], cols_back[...])
        for s in range(each):
            one = None
            two = None
            for j in range(3):
                f = 3 * s + j
                pupil = pupils[group, f]
                rows = back[f * K : (f + 1) * K]
                plain = pupil * rows[:, :GRID]
                cross = pupil * rows[:, GRID:]
                one = plain if one is None else one + plain
                two = cross if two is None else two + cross
            wide[:, :GRID] += weight[group, s] * one
            wide[:, GRID:] += weight[group, s] * two
        return carry

    lax.fori_loop(0, groups, backward, 0)
    scale = norm * 2.0 / (groups * each * K * K)
    one = wide[:, :GRID] * scale
    two = wide[:, GRID:] * scale
    real = one + pltpu.roll(one, K, 1)
    imag = two - pltpu.roll(two, K, 1)
    grad_out[:K] = jnp.where(left, real, -imag)
    for s in range(each):
        term = jnp.sum(rho * powers[0, s], axis=0, keepdims=True)
        grad_out[K + s : K + s + 1] = term * (1.0 / (K * K))


def image_kernel(image, lift_rows, lift_cols, out):
    rows = dot_wide(lift_rows[...], image[...])
    out[0] = wide_dot(rows, lift_cols[...])


def mask_kernel(mine, theirs, back_rows, col_fwd_t, out, source_out, *, pixels):
    each = source_out.shape[0]
    left = lanes((K, GRID)) < K
    parts = []
    for ref in (mine, theirs):
        top = ref[:K]
        turned = pltpu.roll(top, K, 1)
        parts += [top, jnp.where(left, -turned, turned)]
    rows = dot_wide(back_rows[0], jnp.concatenate(parts, 0))
    out[0] = GRAD_SCALE * wide_dot(rows, col_fwd_t[...])
    for s in range(each):
        source_out[s] = jnp.sum(mine[K + s] + theirs[K + s]) * (1.0 / pixels)


def call(body, out_shape, args, **kwargs):
    return pl.pallas_call(body, out_shape=out_shape, **kwargs)(*args)


def body(mask_values, target_image, jones_pupil, polar_states, source_weights, pupil_offsets, polar_ids):
    tile_h, tile_w = mask_values.shape
    each = source_weights.shape[0]
    groups = lax.axis_size("src")
    tiles = lax.axis_size("tile")
    share = tile_h // groups
    tab = make_tables(tile_h, tile_w, tiles)
    vm = pl.BlockSpec(memory_space=pltpu.VMEM)
    sm = pl.BlockSpec(memory_space=pltpu.SMEM)
    tile = lax.axis_index("tile")
    src = lax.axis_index("src")

    edge = jnp.where(tile == 0, mask_values[tile_h - AMB :], mask_values[:AMB])
    halo = flip(edge, "tile", 1)

    known = jnp.concatenate(
        [
            source_weights[None],
            pupil_offsets.reshape(1, 2 * each).astype(F32),
            polar_ids[None].astype(F32),
        ],
        1,
    )
    step = 1
    while step < groups:
        known = jnp.concatenate([known, flip(known, "src", step if step < 4 else 2 * step - 2)], 0)
        step *= 2
    weight = known[:, :each]
    offset = known[:, each : 3 * each].astype(jnp.int32)
    state = known[:, 3 * each :].astype(jnp.int32)

    count = 3 * each
    image, grad = pl.pallas_call(
        source_kernel,
        out_shape=(
            jax.ShapeDtypeStruct((GRID, GRID), F32),
            jax.ShapeDtypeStruct((K + 8 * pl.cdiv(each, 8), GRID), F32),
        ),
        in_specs=[sm] * 5 + [vm] * 14,
        out_specs=(vm, vm),
        scratch_shapes=[
            pltpu.VMEM((6 * polar_states.shape[0], GRID, GRID), F32),
            pltpu.VMEM((groups, count, K, GRID), F32),
            pltpu.VMEM((count * K, 2 * GRID), BF16),
            pltpu.VMEM((groups, 2 * GRID, count * GRID), BF16),
            pltpu.VMEM((groups, each, GRID, GRID), F32),
            pltpu.VMEM((GRID, GRID), F32),
            pltpu.VMEM((GRID, count * GRID), BF16),
            pltpu.VMEM((K, 2 * GRID), F32),
        ],
        name="sources",
    )(
        weight, offset, state, polar_states.reshape(-1), tile.reshape(1).astype(jnp.int32),
        mask_values, halo, target_image, jones_pupil.reshape(12, GRID, GRID),
        tab["col_fwd"], tab["row_core"], tab["row_halo"], tab["cols_out"], tab["rows_out"],
        tab["rows_back"], tab["cols_back"], tab["lift_rows_t"], tab["lift_cols_t"], tab["gram"],
    )

    theirs = flip(grad, "tile", 1)
    rows = lax.dynamic_slice_in_dim(jnp.asarray(tab["lift_rows"]), src * share, share, 0)
    own_image = pl.pallas_call(
        image_kernel,
        out_shape=jax.ShapeDtypeStruct((1, share, tile_w), F32),
        in_specs=[vm] * 3,
        out_specs=vm,
        name="image",
    )(image, rows, tab["lift_cols"])
    back_rows = lax.dynamic_slice(
        jnp.asarray(tab["back_rows"]), (tile, src * share, 0), (1, share, 4 * K)
    )
    own_grad, source_grad = pl.pallas_call(
        lambda *refs: mask_kernel(*refs, pixels=tiles * tile_h * tile_w),
        out_shape=(
            jax.ShapeDtypeStruct((1, share, tile_w), F32),
            jax.ShapeDtypeStruct((each,), F32),
        ),
        in_specs=[vm] * 4,
        out_specs=(vm, sm),
        name="mask",
    )(grad, theirs, back_rows, tab["col_fwd_t"])
    return own_image, own_grad, source_grad


def solution(mesh):
    placed = (
        P(("parts", "tile"), None),
        P(("parts", "tile"), None),
        P(),
        P(),
        P(("parts", "src")),
        P(("parts", "src"), None),
        P(("parts", "src")),
    )
    return jax.shard_map(
        body,
        mesh=mesh,
        in_specs=placed,
        out_specs=(
            P(("parts", "tile"), "src", None),
            P(("parts", "tile"), "src", None),
            P(("parts", "src")),
        ),
        check_vma=False,
    )
```

```python
import math

import jax
import jax.numpy as jnp
import numpy as np
from jax import lax
from jax.experimental import pallas as pl
from jax.experimental.pallas import tpu as pltpu
from jax.sharding import PartitionSpec as P

AMB = 64
K = 64
GRID = 2 * K
GRAD_SCALE = 32.0
F32 = jnp.float32
BF16 = jnp.bfloat16


def flip(value, axis, mask):
    pairs = [(i, i ^ mask) for i in range(lax.axis_size(axis))]
    return lax.ppermute(value, axis, pairs)


def narrow(table):
    return np.asarray(table, np.float32).astype(jnp.bfloat16)


def split(table):
    high = narrow(table)
    return high, narrow(np.asarray(table, np.float64) - high.astype(np.float64))


def kernel_of_orders(gap):
    orders = np.arange(1, K)
    return (1.0 + 2.0 * np.cos(gap[..., None] * orders).sum(-1)) / GRID


def make_tables(tile_h, tile_w, tiles):
    window = tile_h + 2 * AMB
    two_pi = 2.0 * math.pi
    orders = np.arange(K) - K // 2
    cols = np.arange(tile_w)
    rows = np.arange(window)
    points = np.arange(GRID)
    col = two_pi * np.mod(cols[:, None] * orders[None], tile_w) / tile_w
    row = two_pi * np.mod(orders[:, None] * rows[None], window) / window
    grid = two_pi * np.mod(orders[:, None] * points[None], GRID) / GRID
    cos, sin = np.cos(grid), np.sin(grid)
    col_fwd = np.concatenate([np.cos(col), -np.sin(col)], 1)
    row_fwd = np.concatenate([np.cos(row), np.sin(row)], 0)
    cols_out = np.block([[cos, sin], [-cos, -sin], [-sin, cos], [-sin, cos]])
    rows_out = np.block([[cos.T, -sin.T], [sin.T, cos.T]])
    cols_back = np.block(
        [[cos.T, -sin.T, -sin.T, cos.T], [sin.T, cos.T, cos.T, sin.T]]
    )
    core = np.arange(tile_h) + AMB
    lift_rows = kernel_of_orders(
        two_pi * (core[:, None] / window - points[None] / GRID)
    )
    lift_cols = kernel_of_orders(
        two_pi * (points[:, None] / GRID - cols[None] / tile_w)
    )
    gram = (tile_w / GRID) * lift_rows.T @ lift_rows
    halo = np.stack([row_fwd[:, tile_h + AMB :], row_fwd[:, :AMB]])
    rim = np.zeros((tiles * tile_h, 2 * K))
    rim[tile_h - AMB : tile_h] = row_fwd[:, :AMB].T
    rim[tile_h : tile_h + AMB] = row_fwd[:, tile_h + AMB :].T
    return dict(
        col_fwd=narrow(col_fwd),
        col_fwd_t=narrow(col_fwd.T),
        row_core=narrow(row_fwd[:, AMB : AMB + tile_h]),
        row_halo=narrow(halo),
        cols_out=narrow(cols_out),
        rows_out=narrow(rows_out),
        rows_back=narrow(rows_out.T),
        cols_back=narrow(cols_back),
        lift_rows=narrow(lift_rows),
        lift_rows_t=narrow(lift_rows.T),
        lift_cols=narrow(lift_cols),
        lift_cols_t=narrow(lift_cols.T),
        gram=np.stack(split(gram)),
        core_t=narrow(row_fwd[:, AMB : AMB + tile_h].T),
        rim_t=narrow(rim),
    )


def dot(a, b):
    return jnp.dot(a, b, preferred_element_type=F32)


def halves(value):
    high = value.astype(BF16)
    return high, (value - high.astype(F32)).astype(BF16)


def dot_wide(table, value):
    high, low = halves(value)
    return dot(table, high) + dot(table, low)


def wide_dot(value, table):
    high, low = halves(value)
    return dot(high, table) + dot(low, table)


def lanes(shape):
    return lax.broadcasted_iota(jnp.int32, shape, 1)


def pupil_kernel(polar, jones, tables):
    for pol in range(polar.shape[2]):
        ar, br, ai, bi = (polar[n // 2, n % 2, pol] for n in range(4))
        for j in range(3):
            real = jones[2 * j] * ar - jones[6 + 2 * j] * ai
            real += jones[2 * j + 1] * br - jones[6 + 2 * j + 1] * bi
            imag = jones[2 * j] * ai + jones[6 + 2 * j] * ar
            imag += jones[2 * j + 1] * bi + jones[6 + 2 * j + 1] * br
            tables[2 * (3 * pol + j)] = real
            tables[2 * (3 * pol + j) + 1] = pltpu.roll(imag, K, 1)


def core_kernel(
    mask, target, col_fwd, row_core, lift_rows_t, lift_cols_t, product, wanted
):
    part = dot(mask[...], col_fwd[...]).astype(BF16)
    seen = dot(lift_rows_t[...], target[...].astype(BF16)).astype(BF16)
    product[...] = dot(row_core[...], part)
    wanted[...] = dot(seen, lift_cols_t[...])


def source_kernel(
    known, place, product, halo, wanted, tables,
    col_fwd, row_halo, cols_out, rows_out, rows_back, cols_back, gram,
    image_out, grad_out,
    pupils, stack_a, stack_b, fields, powers, image, held_a, held_b, wide,
    *, norm,
):
    each = known.shape[1]
    groups = known.shape[0] // 4
    count = 3 * each
    left = lanes((K, GRID)) < K

    edge = dot(halo[...], col_fwd[...]).astype(BF16)
    whole = product[...] + dot(row_halo[place[0]], edge)
    turned = pltpu.roll(whole[K:], K, 1)
    first = norm * (whole[:K] + jnp.where(left, turned, -turned))
    second = pltpu.roll(first, K, 1)

    image[...] = jnp.zeros_like(image)

    def mask_fields(group, stack):
        for s in range(each):
            up = known[4 * group + 1, s].astype(jnp.int32)
            side = known[4 * group + 2, s].astype(jnp.int32)
            pol = known[4 * group + 3, s].astype(jnp.int32)
            inside = (lanes((K, GRID)) >= side) & (lanes((K, GRID)) < side + K)
            turn = jnp.where(side == 0, 0, GRID - side)
            for j in range(3):
                real = tables[2 * (3 * pol + j), pl.ds(up, K), :]
                imag = tables[2 * (3 * pol + j) + 1, pl.ds(up, K), :]
                pupil = pltpu.roll(jnp.where(inside, real, imag), turn, 1)
                f = 3 * s + j
                pupils[group, f] = pupil
                stack[f * K : (f + 1) * K, :GRID] = (pupil * first).astype(BF16)
                stack[f * K : (f + 1) * K, GRID:] = (pupil * second).astype(BF16)

    def columns(stack, held):
        across = dot(stack[...], cols_out[...]).astype(BF16)
        for f in range(count):
            rows = across[f * K : (f + 1) * K]
            held[:K, f * GRID : (f + 1) * GRID] = rows[:, :GRID]
            held[K:, f * GRID : (f + 1) * GRID] = rows[:, GRID:]

    def rows(group, held):
        rated = None
        for s in range(each):
            power = None
            for j in range(3):
                f = 3 * s + j
                field = dot(rows_out[...], held[:, f * GRID : (f + 1) * GRID])
                fields[group, :, f * GRID : (f + 1) * GRID] = field.astype(fields.dtype)
                square = field[:GRID] * field[:GRID] + field[GRID:] * field[GRID:]
                power = square if power is None else power + square
            powers[group, s] = power
            power = known[4 * group, s] * power
            rated = power if rated is None else rated + power
        image[...] += rated

    last = groups - 1
    mask_fields(0, stack_a)
    columns(stack_a, held_a)
    mask_fields(1, stack_b)

    def forward(i, carry):
        rows(2 * i, held_a)
        columns(stack_b, held_b)
        mask_fields(2 * i + 2, stack_a)
        rows(2 * i + 1, held_b)
        columns(stack_a, held_a)
        mask_fields(2 * i + 3, stack_b)
        return carry

    lax.fori_loop(0, groups // 2 - 1, forward, 0)
    rows(last - 1, held_a)
    columns(stack_b, held_b)
    rows(last, held_b)

    total = image[...] * (1.0 / (groups * each * K * K))
    image_out[...] = total

    high, low = halves(total)
    rho = dot(gram[0], high) + dot(gram[0], low) + dot(gram[1], high) - wanted[...]
    double = jnp.concatenate([rho, rho], 0).astype(fields.dtype)

    grad_out[...] = jnp.zeros_like(grad_out)
    wide[...] = jnp.zeros_like(wide)

    def rows_adjoint(group, stack):
        for f in range(0, count, 2):
            pair = [
                fields[group, :, n * GRID : (n + 1) * GRID] * double for n in (f, f + 1)
            ]
            down = dot(rows_back[...], jnp.concatenate(pair, 1).astype(BF16)).astype(BF16)
            for n in (0, 1):
                one = down[:, n * GRID : (n + 1) * GRID]
                stack[(f + n) * K : (f + n + 1) * K, :GRID] = one[:K]
                stack[(f + n) * K : (f + n + 1) * K, GRID:] = one[K:]

    def columns_adjoint(group, stack):
        back = dot(stack[...], cols_back[...])
        first_sum = None
        second_sum = None
        for s in range(each):
            one = None
            two = None
            for j in range(3):
                f = 3 * s + j
                pupil = pupils[group, f]
                part = back[f * K : (f + 1) * K]
                plain = pupil * part[:, :GRID]
                cross = pupil * part[:, GRID:]
                one = plain if one is None else one + plain
                two = cross if two is None else two + cross
            one = known[4 * group, s] * one
            two = known[4 * group, s] * two
            first_sum = one if first_sum is None else first_sum + one
            second_sum = two if second_sum is None else second_sum + two
        wide[:, :GRID] += first_sum
        wide[:, GRID:] += second_sum

    rows_adjoint(0, stack_a)

    def backward(i, carry):
        columns_adjoint(2 * i, stack_a)
        rows_adjoint(2 * i + 1, stack_b)
        columns_adjoint(2 * i + 1, stack_b)
        rows_adjoint(2 * i + 2, stack_a)
        return carry

    lax.fori_loop(0, groups // 2 - 1, backward, 0)
    columns_adjoint(last - 1, stack_a)
    rows_adjoint(last, stack_b)
    columns_adjoint(last, stack_b)

    scale = norm * 2.0 / (groups * each * K * K)
    one = wide[:, :GRID] * scale
    two = wide[:, GRID:] * scale
    real = one + pltpu.roll(one, K, 1)
    imag = two - pltpu.roll(two, K, 1)
    grad_out[:K] = jnp.where(left, real, -imag)
    for s in range(each):
        term = jnp.sum(rho * powers[0, s], axis=0, keepdims=True)
        grad_out[K + s : K + s + 1] = term * (1.0 / (K * K))


def own(table, start, share):
    return table[pl.ds(pl.multiple_of(start, share), share), :]


def image_kernel(place, image, lift_rows, lift_cols, out):
    rows = dot_wide(own(lift_rows, place[1], out.shape[1]), image[...])
    out[0] = wide_dot(rows, lift_cols[...])


def mask_kernel(place, mine, theirs, core_t, rim_t, col_fwd_t, out, source_out, *, pixels):
    each = source_out.shape[0]
    share = out.shape[1]
    left = lanes((K, GRID)) < K
    rows = 0.0
    for ref, table, start in (
        (mine, core_t, place[1]),
        (theirs, rim_t, place[0] * core_t.shape[0] + place[1]),
    ):
        top = ref[:K]
        turned = pltpu.roll(top, K, 1)
        both = jnp.concatenate([top, jnp.where(left, -turned, turned)], 0)
        rows += dot_wide(own(table, start, share), both)
    out[0] = GRAD_SCALE * wide_dot(rows, col_fwd_t[...])
    for s in range(each):
        source_out[s] = jnp.sum(mine[K + s] + theirs[K + s]) * (1.0 / pixels)


def pack_kernel(weight, offset, state, out):
    out[0:1] = weight[...]
    out[1:3] = offset[...].astype(F32)
    out[3:4] = state[...].astype(F32)


LARGE = 48 << 20
VM = pl.BlockSpec(memory_space=pltpu.VMEM)
SM = pl.BlockSpec(memory_space=pltpu.SMEM)


def run(name, kernel, out_shape, scalars, arrays, out_specs, flops, scratch=(), held=0):
    outs = out_shape if isinstance(out_shape, tuple) else (out_shape,)
    size = held + sum(a.size * a.dtype.itemsize for a in (*arrays, *outs))
    return pl.pallas_call(
        kernel,
        out_shape=out_shape,
        in_specs=[SM] * len(scalars) + [VM] * len(arrays),
        out_specs=out_specs,
        scratch_shapes=scratch,
        compiler_params=pltpu.CompilerParams(vmem_limit_bytes=size + (6 << 20)),
        cost_estimate=pl.CostEstimate(flops=flops, bytes_accessed=size, transcendentals=0),
        name=name,
    )(*scalars, *arrays)


def body(mask_values, target_image, jones_pupil, polar_states, source_weights, pupil_offsets, polar_ids):
    tile_h, tile_w = mask_values.shape
    each = source_weights.shape[0]
    groups = lax.axis_size("src")
    tiles = lax.axis_size("tile")
    share = tile_h // groups
    tab = make_tables(tile_h, tile_w, tiles)
    tile = lax.axis_index("tile")
    src = lax.axis_index("src")
    place = jnp.stack([tile, src * share]).astype(jnp.int32)
    shape = jax.ShapeDtypeStruct

    known = run(
        "pack", pack_kernel, shape((4, each), F32), [],
        [source_weights[None], pupil_offsets.T, polar_ids[None]], VM, flops=1, held=LARGE,
    )
    step = 1
    while step < groups:
        known = jnp.concatenate([known, flip(known, "src", step)], 0)
        step *= 2
    edge = jnp.where(tile == 0, mask_values[tile_h - AMB :], mask_values[:AMB])
    halo = flip(edge, "tile", 1)

    pols = polar_states.shape[0]
    tables = run(
        "pupils", pupil_kernel, shape((6 * pols, GRID, GRID), F32),
        [polar_states.transpose(1, 2, 0)], [jones_pupil.reshape(12, GRID, GRID)], VM,
        flops=48 * pols * GRID * GRID, held=LARGE,
    )
    product, wanted = run(
        "core", core_kernel, (shape((2 * K, 2 * K), F32), shape((GRID, GRID), F32)), [],
        [mask_values, target_image]
        + [tab[n] for n in ("col_fwd", "row_core", "lift_rows_t", "lift_cols_t")],
        (VM, VM), flops=2**28, held=LARGE,
    )
    count = 3 * each
    scratch = [
        ((groups, count, K, GRID), F32),
        ((count * K, 2 * GRID), BF16),
        ((count * K, 2 * GRID), BF16),
        ((groups, 2 * GRID, count * GRID), F32 if groups * each <= 64 else BF16),
        ((groups, each, GRID, GRID), F32),
        ((GRID, GRID), F32),
        ((GRID, count * GRID), BF16),
        ((GRID, count * GRID), BF16),
        ((K, 2 * GRID), F32),
    ]
    norm = 1.0 / math.sqrt((tile_h + 2 * AMB) * tile_w)
    image, grad = run(
        "sources", lambda *refs: source_kernel(*refs, norm=norm),
        (shape((GRID, GRID), F32), shape((K + 8 * pl.cdiv(each, 8), GRID), F32)),
        [known, place], [product, halo, wanted, tables]
        + [tab[n] for n in ("col_fwd", "row_halo", "cols_out", "rows_out", "rows_back", "cols_back", "gram")],
        (VM, VM), flops=2**32,
        scratch=[pltpu.VMEM(*s) for s in scratch],
        held=sum(math.prod(s) * jnp.dtype(d).itemsize for s, d in scratch),
    )
    theirs = flip(grad, "tile", 1)
    own_image = run(
        "image", image_kernel, shape((1, share, tile_w), F32), [place],
        [image, tab["lift_rows"], tab["lift_cols"]], VM, flops=2**24,
    )
    own_grad, source_grad = run(
        "mask", lambda *refs: mask_kernel(*refs, pixels=tiles * tile_h * tile_w),
        (shape((1, share, tile_w), F32), shape((each,), F32)), [place],
        [grad, theirs, tab["core_t"], tab["rim_t"], tab["col_fwd_t"]],
        (VM, SM), flops=2**24,
    )
    return own_image, own_grad, source_grad


def solution(mesh):
    placed = (
        P(("parts", "tile"), None),
        P(("parts", "tile"), None),
        P(),
        P(),
        P(("parts", "src")),
        P(("parts", "src"), None),
        P(("parts", "src")),
    )
    return jax.shard_map(
        body,
        mesh=mesh,
        in_specs=placed,
        out_specs=(
            P(("parts", "tile"), "src", None),
            P(("parts", "tile"), "src", None),
            P(("parts", "src")),
        ),
        check_vma=False,
    )
```

```python
import math

import jax
import jax.numpy as jnp
import numpy as np
from jax import lax
from jax.experimental import pallas as pl
from jax.experimental.pallas import tpu as pltpu
from jax.sharding import PartitionSpec as P

AMB = 64
K = 64
GRID = 2 * K
GRAD_SCALE = 32.0
F32 = jnp.float32
BF16 = jnp.bfloat16


def flip(value, axis, mask):
    pairs = [(i, i ^ mask) for i in range(lax.axis_size(axis))]
    return lax.ppermute(value, axis, pairs)


def narrow(table):
    return np.asarray(table, np.float32).astype(jnp.bfloat16)


def split(table):
    high = narrow(table)
    return high, narrow(np.asarray(table, np.float64) - high.astype(np.float64))


def kernel_of_orders(gap):
    orders = np.arange(1, K)
    return (1.0 + 2.0 * np.cos(gap[..., None] * orders).sum(-1)) / GRID


def make_tables(tile_h, tile_w, tiles):
    window = tile_h + 2 * AMB
    two_pi = 2.0 * math.pi
    orders = np.arange(K) - K // 2
    cols = np.arange(tile_w)
    rows = np.arange(window)
    points = np.arange(GRID)
    col = two_pi * np.mod(cols[:, None] * orders[None], tile_w) / tile_w
    row = two_pi * np.mod(orders[:, None] * rows[None], window) / window
    grid = two_pi * np.mod(orders[:, None] * points[None], GRID) / GRID
    cos, sin = np.cos(grid), np.sin(grid)
    col_fwd = np.concatenate([np.cos(col), -np.sin(col)], 1)
    row_fwd = np.concatenate([np.cos(row), np.sin(row)], 0)
    cols_out = np.block([[cos, sin], [-cos, -sin], [-sin, cos], [-sin, cos]])
    rows_out = np.block([[cos.T, -sin.T], [sin.T, cos.T]])
    cols_back = np.block(
        [[cos.T, -sin.T, -sin.T, cos.T], [sin.T, cos.T, cos.T, sin.T]]
    )
    core = np.arange(tile_h) + AMB
    lift_rows = kernel_of_orders(
        two_pi * (core[:, None] / window - points[None] / GRID)
    )
    lift_cols = kernel_of_orders(
        two_pi * (points[:, None] / GRID - cols[None] / tile_w)
    )
    gram = (tile_w / GRID) * lift_rows.T @ lift_rows
    halo = np.stack([row_fwd[:, tile_h + AMB :], row_fwd[:, :AMB]])
    rim = np.zeros((tiles * tile_h, 2 * K))
    rim[tile_h - AMB : tile_h] = row_fwd[:, :AMB].T
    rim[tile_h : tile_h + AMB] = row_fwd[:, tile_h + AMB :].T
    return dict(
        col_fwd=narrow(col_fwd),
        col_fwd_t=narrow(col_fwd.T),
        row_core=narrow(row_fwd[:, AMB : AMB + tile_h]),
        row_halo=narrow(halo),
        cols_out=narrow(cols_out),
        rows_out=narrow(rows_out),
        rows_back=narrow(rows_out.T),
        cols_back=narrow(cols_back),
        lift_rows=narrow(lift_rows),
        lift_rows_t=narrow(lift_rows.T),
        lift_cols=narrow(lift_cols),
        lift_cols_t=narrow(lift_cols.T),
        gram=np.stack(split(gram)),
        core_t=narrow(row_fwd[:, AMB : AMB + tile_h].T),
        rim_t=narrow(rim),
    )


def dot(a, b):
    return jnp.dot(a, b, preferred_element_type=F32)


def halves(value):
    high = value.astype(BF16)
    return high, (value - high.astype(F32)).astype(BF16)


def dot_wide(table, value):
    high, low = halves(value)
    return dot(table, high) + dot(table, low)


def wide_dot(value, table):
    high, low = halves(value)
    return dot(high, table) + dot(low, table)


def lanes(shape):
    return lax.broadcasted_iota(jnp.int32, shape, 1)


def pupil_kernel(polar, jones, tables):
    for pol in range(polar.shape[2]):
        ar, br, ai, bi = (polar[n // 2, n % 2, pol] for n in range(4))
        for j in range(3):
            real = jones[2 * j] * ar - jones[6 + 2 * j] * ai
            real += jones[2 * j + 1] * br - jones[6 + 2 * j + 1] * bi
            imag = jones[2 * j] * ai + jones[6 + 2 * j] * ar
            imag += jones[2 * j + 1] * bi + jones[6 + 2 * j + 1] * br
            tables[2 * (3 * pol + j)] = real
            tables[2 * (3 * pol + j) + 1] = pltpu.roll(imag, K, 1)


def fetch(pairs, sems):
    copies = [pltpu.make_async_copy(a, b, sems.at[n]) for n, (a, b) in enumerate(pairs)]
    for copy in copies:
        copy.start()
    return copies


def core_kernel(
    place, mask_far, col_far, row_far, product, edge, mask, col_fwd, row_core, sems
):
    copies = fetch([(col_far, col_fwd), (mask_far, mask), (row_far, row_core)], sems)
    copies[0].wait()
    copies[1].wait()
    start = (1 - place[0]) * (mask.shape[0] - AMB)
    edge[...] = mask[pl.ds(pl.multiple_of(start, AMB), AMB), :]
    part = dot(mask[...], col_fwd[...]).astype(BF16)
    copies[2].wait()
    product[...] = dot(row_core[...], part)


def target_kernel(
    target_far, rows_far, cols_far, wanted, target, lift_rows_t, lift_cols_t, sems
):
    pairs = [(target_far, target), (rows_far, lift_rows_t), (cols_far, lift_cols_t)]
    for copy in fetch(pairs, sems):
        copy.wait()
    seen = dot(lift_rows_t[...], target[...].astype(BF16)).astype(BF16)
    wanted[...] = dot(seen, lift_cols_t[...])


def source_kernel(
    known, place, product, halo, wanted, tables,
    col_fwd, row_halo, cols_out, rows_out, rows_back, cols_back, gram,
    image_out, grad_out,
    pupils, fields, powers, image, wide, *buffers,
    norm,
):
    each = known.shape[1]
    groups = known.shape[0] // 4
    units, count = fields.shape[:2]
    unit = count // 3
    even, odd = buffers[:3], buffers[3:]
    left = lanes((K, GRID)) < K

    edge = dot(halo[...], col_fwd[...]).astype(BF16)
    whole = product[...] + dot(row_halo[place[0]], edge)
    turned = pltpu.roll(whole[K:], K, 1)
    first = norm * (whole[:K] + jnp.where(left, turned, -turned))
    second = pltpu.roll(first, K, 1)

    image[...] = jnp.zeros_like(image)

    def value(row, u, s):
        n = u * unit + s
        group = lax.div(n, each)
        return known[4 * group + row, n - group * each]

    def mask_fields(u, buffer):
        for s in range(unit):
            up, side, pol = (value(row, u, s).astype(jnp.int32) for row in (1, 2, 3))
            inside = (lanes((K, GRID)) >= side) & (lanes((K, GRID)) < side + K)
            turn = jnp.where(side == 0, 0, GRID - side)
            for j in range(3):
                real = tables[2 * (3 * pol + j), pl.ds(up, K), :]
                imag = tables[2 * (3 * pol + j) + 1, pl.ds(up, K), :]
                pupil = pltpu.roll(jnp.where(inside, real, imag), turn, 1)
                f = 3 * s + j
                pupils[u, f] = pupil
                buffer[0][f * K : (f + 1) * K] = (pupil * first).astype(BF16)
                buffer[1][f * K : (f + 1) * K] = (pupil * second).astype(BF16)

    def columns(buffer):
        both = jnp.concatenate([buffer[0][...], buffer[1][...]], 1)
        across = dot(both, cols_out[...]).astype(BF16)
        for f in range(count):
            part = across[f * K : (f + 1) * K]
            buffer[2][f, :K] = part[:, :GRID]
            buffer[2][f, K:] = part[:, GRID:]

    def rows(u, buffer):
        rated = None
        for s in range(unit):
            power = None
            for j in range(3):
                f = 3 * s + j
                field = dot(rows_out[...], buffer[2][f])
                fields[u, f] = field.astype(fields.dtype)
                square = field[:GRID] * field[:GRID] + field[GRID:] * field[GRID:]
                power = square if power is None else power + square
            powers[u, s] = power
            power = value(0, u, s) * power
            rated = power if rated is None else rated + power
        image[...] += rated

    last = units - 1
    mask_fields(0, even)
    columns(even)
    mask_fields(1, odd)

    def forward(u):
        rows(u, even)
        columns(odd)
        mask_fields(u + 2, even)
        rows(u + 1, odd)
        columns(even)
        mask_fields(u + 3, odd)

    def forward_pair(i, carry):
        forward(2 * i)
        return carry

    lax.fori_loop(0, units // 2 - 1, forward_pair, 0)
    rows(last - 1, even)
    columns(odd)
    rows(last, odd)

    total = image[...] * (1.0 / (groups * each * K * K))
    image_out[...] = total

    high, low = halves(total)
    rho = dot(gram[0], high) + dot(gram[0], low) + dot(gram[1], high) - wanted[...]
    double = jnp.concatenate([rho, rho], 0).astype(fields.dtype)

    grad_out[K:] = jnp.zeros_like(grad_out[K:])
    wide[...] = jnp.zeros_like(wide)

    def rows_adjoint(u, buffer):
        for f in range(0, count, 2):
            pair = [fields[u, n] * double for n in (f, f + 1)]
            down = dot(rows_back[...], jnp.concatenate(pair, 1).astype(BF16)).astype(BF16)
            for n in (0, 1):
                one = down[:, n * GRID : (n + 1) * GRID]
                buffer[0][(f + n) * K : (f + n + 1) * K] = one[:K]
                buffer[1][(f + n) * K : (f + n + 1) * K] = one[K:]

    def columns_adjoint(u, buffer):
        both = jnp.concatenate([buffer[0][...], buffer[1][...]], 1)
        back = dot(both, cols_back[...])
        plain_sum = None
        cross_sum = None
        for s in range(unit):
            one = None
            two = None
            for j in range(3):
                f = 3 * s + j
                pupil = pupils[u, f]
                part = back[f * K : (f + 1) * K]
                plain = pupil * part[:, :GRID]
                cross = pupil * part[:, GRID:]
                one = plain if one is None else one + plain
                two = cross if two is None else two + cross
            one = value(0, u, s) * one
            two = value(0, u, s) * two
            plain_sum = one if plain_sum is None else plain_sum + one
            cross_sum = two if cross_sum is None else cross_sum + two
        wide[:, :GRID] += plain_sum
        wide[:, GRID:] += cross_sum

    rows_adjoint(0, even)

    def backward(u):
        columns_adjoint(u, even)
        rows_adjoint(u + 1, odd)
        columns_adjoint(u + 1, odd)
        rows_adjoint(u + 2, even)

    def backward_pair(i, carry):
        backward(2 * i)
        return carry

    lax.fori_loop(0, units // 2 - 1, backward_pair, 0)
    columns_adjoint(last - 1, even)
    rows_adjoint(last, odd)
    columns_adjoint(last, odd)

    scale = norm * 2.0 / (groups * each * K * K)
    one = wide[:, :GRID] * scale
    two = wide[:, GRID:] * scale
    real = one + pltpu.roll(one, K, 1)
    imag = two - pltpu.roll(two, K, 1)
    grad_out[:K] = jnp.where(left, real, -imag)
    terms = jnp.zeros((1, GRID), F32)
    for s in range(each):
        power = powers[s // unit, s % unit]
        term = jnp.sum(jnp.sum(rho * power, 0, keepdims=True), 1, keepdims=True)
        terms = jnp.where(lanes((1, GRID)) == s, term * (1.0 / (K * K)), terms)
    grad_out[K : K + 1] = terms


def own(table, start, share):
    return table[pl.ds(pl.multiple_of(start, share), share), :]


def image_kernel(place, image, lift_rows, lift_cols, out):
    rows = dot_wide(own(lift_rows, place[1], out.shape[1]), image[...])
    out[0] = wide_dot(rows, lift_cols[...])


def mask_kernel(place, mine, theirs, core_t, rim_t, col_fwd_t, out, source_out, *, pixels):
    each = source_out.shape[1]
    share = out.shape[1]
    left = lanes((K, GRID)) < K
    rows = 0.0
    for ref, table, start in (
        (mine, core_t, place[1]),
        (theirs, rim_t, place[0] * core_t.shape[0] + place[1]),
    ):
        top = ref[:K]
        turned = pltpu.roll(top, K, 1)
        both = jnp.concatenate([top, jnp.where(left, -turned, turned)], 0)
        rows += dot_wide(own(table, start, share), both)
    out[0] = GRAD_SCALE * wide_dot(rows, col_fwd_t[...])
    terms = mine[K : K + 1] + theirs[K : K + 1]
    source_out[...] = terms[:, :each] * (1.0 / pixels)


def pack_kernel(weight_far, offset_far, state_far, out, weight, offset, state, sems):
    pairs = [(weight_far, weight), (offset_far, offset), (state_far, state)]
    for copy in fetch(pairs, sems):
        copy.wait()
    out[0:1] = weight[...]
    out[1:3] = offset[...].astype(F32)
    out[3:4] = state[...].astype(F32)


FAR = pl.BlockSpec(memory_space=pltpu.HBM)
VM = pl.BlockSpec(memory_space=pltpu.VMEM)
SM = pl.BlockSpec(memory_space=pltpu.SMEM)


def run(name, kernel, out_shape, scalars, arrays, flops, scratch=(), held=0, far=False):
    outs = out_shape if isinstance(out_shape, tuple) else (out_shape,)
    if far:
        scratch = [pltpu.VMEM(a.shape, a.dtype) for a in arrays]
        scratch.append(pltpu.SemaphoreType.DMA((len(arrays),)))
        arrays = [pltpu.with_memory_space_constraint(a, pltpu.HBM) for a in arrays]
    size = held + sum(a.size * a.dtype.itemsize for a in (*arrays, *outs))
    return pl.pallas_call(
        kernel,
        out_shape=out_shape,
        in_specs=[SM] * len(scalars) + [FAR if far else VM] * len(arrays),
        out_specs=jax.tree.map(lambda _: VM, out_shape),
        scratch_shapes=scratch,
        compiler_params=pltpu.CompilerParams(vmem_limit_bytes=size + (4 << 20)),
        cost_estimate=pl.CostEstimate(flops=flops, bytes_accessed=size, transcendentals=0),
        name=name,
    )(*scalars, *arrays)


def body(mask_values, target_image, jones_pupil, polar_states, source_weights, pupil_offsets, polar_ids):
    tile_h, tile_w = mask_values.shape
    each = source_weights.shape[0]
    groups = lax.axis_size("src")
    tiles = lax.axis_size("tile")
    share = tile_h // groups
    tab = make_tables(tile_h, tile_w, tiles)
    tile = lax.axis_index("tile")
    src = lax.axis_index("src")
    place = jnp.stack([tile, src * share]).astype(jnp.int32)
    shape = jax.ShapeDtypeStruct

    known = run(
        "pack", pack_kernel, shape((4, each), F32), [],
        [source_weights[None], pupil_offsets.T, polar_ids[None]], flops=1, far=True,
    )
    step = 1
    while step < groups:
        known = jnp.concatenate([known, flip(known, "src", step)], 0)
        step *= 2

    product, edge = run(
        "core", core_kernel, (shape((2 * K, 2 * K), F32), shape((AMB, tile_w), BF16)),
        [place], [mask_values, tab["col_fwd"], tab["row_core"]], flops=2**27, far=True,
    )
    halo = flip(edge, "tile", 1)
    wanted = run(
        "target", target_kernel, shape((GRID, GRID), F32), [],
        [target_image, tab["lift_rows_t"], tab["lift_cols_t"]],
        flops=2**27, far=True,
    )
    pols = polar_states.shape[0]
    tables = run(
        "pupils", pupil_kernel, shape((6 * pols, GRID, GRID), F32),
        [polar_states.transpose(1, 2, 0)], [jones_pupil.reshape(12, GRID, GRID)],
        flops=48 * pols * GRID * GRID,
    )
    unit = each
    units = groups
    count = 3 * unit
    shapes = [
        ((units, count, K, GRID), F32),
        ((units, count, 2 * GRID, GRID), F32 if groups * each <= 64 else BF16),
        ((units, unit, GRID, GRID), F32),
        ((GRID, GRID), F32),
        ((K, 2 * GRID), F32),
    ]
    shapes += 2 * [
        ((count * K, GRID), BF16),
        ((count * K, GRID), BF16),
        ((count, GRID, GRID), BF16),
    ]
    norm = 1.0 / math.sqrt((tile_h + 2 * AMB) * tile_w)
    image, grad = run(
        "sources", lambda *refs: source_kernel(*refs, norm=norm),
        (shape((GRID, GRID), F32), shape((K + 8, GRID), F32)),
        [known, place], [product, halo, wanted, tables]
        + [tab[n] for n in ("col_fwd", "row_halo", "cols_out", "rows_out", "rows_back", "cols_back", "gram")],
        flops=2**32,
        scratch=[pltpu.VMEM(*s) for s in shapes],
        held=sum(math.prod(s) * jnp.dtype(d).itemsize for s, d in shapes),
    )
    theirs = flip(grad, "tile", 1)
    own_image = run(
        "image", image_kernel, shape((1, share, tile_w), F32), [place],
        [image, tab["lift_rows"], tab["lift_cols"]], flops=2**24,
    )
    own_grad, source_grad = run(
        "mask", lambda *refs: mask_kernel(*refs, pixels=tiles * tile_h * tile_w),
        (shape((1, share, tile_w), F32), shape((1, each), F32)), [place],
        [grad, theirs, tab["core_t"], tab["rim_t"], tab["col_fwd_t"]], flops=2**24,
    )
    return own_image, own_grad, source_grad.reshape(each)


def solution(mesh):
    placed = (
        P(("parts", "tile"), None),
        P(("parts", "tile"), None),
        P(),
        P(),
        P(("parts", "src")),
        P(("parts", "src"), None),
        P(("parts", "src")),
    )
    return jax.shard_map(
        body,
        mesh=mesh,
        in_specs=placed,
        out_specs=(
            P(("parts", "tile"), "src", None),
            P(("parts", "tile"), "src", None),
            P(("parts", "src")),
        ),
        check_vma=False,
    )
```

```python
import math

import jax
import jax.numpy as jnp
import numpy as np
from jax import lax
from jax.experimental import pallas as pl
from jax.experimental.pallas import tpu as pltpu
from jax.sharding import PartitionSpec as P


AMB = 64
K = 64
GRID = 2 * K
GRAD_SCALE = 32.0
F32 = jnp.float32
BF16 = jnp.bfloat16


def flip(value, axis, mask):
    pairs = [(i, i ^ mask) for i in range(lax.axis_size(axis))]
    return lax.ppermute(value, axis, pairs)


def narrow(table):
    return np.asarray(table, np.float32).astype(jnp.bfloat16)


def split(table):
    high = narrow(table)
    return high, narrow(np.asarray(table, np.float64) - high.astype(np.float64))


def kernel_of_orders(gap):
    orders = np.arange(1, K)
    return (1.0 + 2.0 * np.cos(gap[..., None] * orders).sum(-1)) / GRID


def make_tables(tile_h, tile_w, tiles):
    window = tile_h + 2 * AMB
    two_pi = 2.0 * math.pi
    orders = np.arange(K) - K // 2
    cols = np.arange(tile_w)
    rows = np.arange(window)
    points = np.arange(GRID)
    col = two_pi * np.mod(cols[:, None] * orders[None], tile_w) / tile_w
    row = two_pi * np.mod(orders[:, None] * rows[None], window) / window
    grid = two_pi * np.mod(orders[:, None] * points[None], GRID) / GRID
    cos, sin = np.cos(grid), np.sin(grid)
    col_fwd = np.concatenate([np.cos(col), -np.sin(col)], 1)
    row_fwd = np.concatenate([np.cos(row), np.sin(row)], 0)
    cols_out = np.block([[cos, sin], [-cos, -sin], [-sin, cos], [-sin, cos]])
    rows_out = np.block([[cos.T, -sin.T], [sin.T, cos.T]])
    cols_back = np.block(
        [[cos.T, -sin.T, -sin.T, cos.T], [sin.T, cos.T, cos.T, sin.T]]
    )
    core = np.arange(tile_h) + AMB
    lift_rows = kernel_of_orders(
        two_pi * (core[:, None] / window - points[None] / GRID)
    )
    lift_cols = kernel_of_orders(
        two_pi * (points[:, None] / GRID - cols[None] / tile_w)
    )
    gram = (tile_w / GRID) * lift_rows.T @ lift_rows
    halo = np.stack([row_fwd[:, tile_h + AMB :], row_fwd[:, :AMB]])
    rim = np.zeros((tiles * tile_h, 2 * K))
    rim[tile_h - AMB : tile_h] = row_fwd[:, :AMB].T
    rim[tile_h : tile_h + AMB] = row_fwd[:, tile_h + AMB :].T
    return dict(
        col_fwd=narrow(col_fwd),
        col_fwd_t=narrow(col_fwd.T),
        row_core=narrow(row_fwd[:, AMB : AMB + tile_h]),
        row_halo=narrow(halo),
        cols_out=narrow(cols_out),
        rows_out=narrow(rows_out),
        rows_back=narrow(rows_out.T),
        cols_back=narrow(cols_back),
        lift_rows=narrow(lift_rows),
        lift_rows_t=narrow(lift_rows.T),
        lift_cols=narrow(lift_cols),
        lift_cols_t=narrow(lift_cols.T),
        gram=np.stack(split(gram)),
        core_t=narrow(row_fwd[:, AMB : AMB + tile_h].T),
        rim_t=narrow(rim),
    )


def dot(a, b):
    return jnp.dot(a, b, preferred_element_type=F32)


def halves(value):
    high = value.astype(BF16)
    return high, (value - high.astype(F32)).astype(BF16)


def dot_wide(table, value):
    high, low = halves(value)
    return dot(table, high) + dot(table, low)


def wide_dot(value, table):
    high, low = halves(value)
    return dot(high, table) + dot(low, table)


def lanes(shape):
    return lax.broadcasted_iota(jnp.int32, shape, 1)


def prepare_kernel(
    polar, jones, part, halo, col_fwd, row_core, row_halo, tables, spectrum, *, norm
):
    left = lanes((K, GRID)) < K
    edge = dot(halo[...], col_fwd[...]).astype(BF16)
    whole = dot(row_core[...], part[...]) + dot(row_halo[lax.axis_index("tile")], edge)
    turned = pltpu.roll(whole[K:], K, 1)
    spectrum[...] = norm * (whole[:K] + jnp.where(left, turned, -turned))
    for pol in range(polar.shape[2]):
        ar, br, ai, bi = (polar[n // 2, n % 2, pol] for n in range(4))
        for j in range(3):
            real = jones[2 * j] * ar - jones[6 + 2 * j] * ai
            real += jones[2 * j + 1] * br - jones[6 + 2 * j + 1] * bi
            imag = jones[2 * j] * ai + jones[6 + 2 * j] * ar
            imag += jones[2 * j + 1] * bi + jones[6 + 2 * j + 1] * br
            tables[2 * (3 * pol + j)] = real
            tables[2 * (3 * pol + j) + 1] = pltpu.roll(imag, K, 1)


def fetch(pairs, sems):
    copies = [pltpu.make_async_copy(a, b, sems.at[n]) for n, (a, b) in enumerate(pairs)]
    for copy in copies:
        copy.start()
    return copies


def core_kernel(mask_far, col_far, part, edge, mask, col_fwd, sems):
    copies = fetch([(mask_far, mask), (col_far, col_fwd)], sems)
    for copy in copies:
        copy.wait()
    start = (1 - lax.axis_index("tile")) * (mask.shape[0] - AMB)
    edge[...] = mask[pl.ds(pl.multiple_of(start, AMB), AMB), :]
    part[...] = dot(mask[...], col_fwd[...]).astype(BF16)


def target_kernel(
    target_far, rows_far, cols_far, wanted, target, lift_rows_t, lift_cols_t, sems
):
    pairs = [(target_far, target), (rows_far, lift_rows_t), (cols_far, lift_cols_t)]
    for copy in fetch(pairs, sems):
        copy.wait()
    seen = dot(lift_rows_t[...], target[...].astype(BF16)).astype(BF16)
    wanted[...] = dot(seen, lift_cols_t[...])


def source_kernel(
    known, spectrum, wanted, tables,
    cols_out, rows_out, rows_back, cols_back, gram,
    image_out, grad_out,
    pupils, fields, powers, image, wide, *buffers,
    norm,
):
    each = known.shape[1]
    groups = known.shape[0] // 4
    units, count = fields.shape[:2]
    unit = count // 3
    even, odd = buffers[:3], buffers[3:]
    left = lanes((K, GRID)) < K

    first = spectrum[...]
    second = pltpu.roll(first, K, 1)

    image[...] = jnp.zeros_like(image)

    def value(row, u, s):
        n = u * unit + s
        group = lax.div(n, each)
        return known[4 * group + row, n - group * each]

    def mask_fields(u, buffer):
        for s in range(unit):
            up, side, pol = (value(row, u, s).astype(jnp.int32) for row in (1, 2, 3))
            inside = (lanes((K, GRID)) >= side) & (lanes((K, GRID)) < side + K)
            turn = jnp.where(side == 0, 0, GRID - side)
            for j in range(3):
                real = tables[2 * (3 * pol + j), pl.ds(up, K), :]
                imag = tables[2 * (3 * pol + j) + 1, pl.ds(up, K), :]
                pupil = pltpu.roll(jnp.where(inside, real, imag), turn, 1)
                f = 3 * s + j
                pupils[u, f] = pupil
                buffer[0][f * K : (f + 1) * K] = (pupil * first).astype(BF16)
                buffer[1][f * K : (f + 1) * K] = (pupil * second).astype(BF16)

    def columns(buffer):
        both = jnp.concatenate([buffer[0][...], buffer[1][...]], 1)
        across = dot(both, cols_out[...]).astype(BF16)
        for f in range(count):
            part = across[f * K : (f + 1) * K]
            buffer[2][f, :K] = part[:, :GRID]
            buffer[2][f, K:] = part[:, GRID:]

    def rows(u, buffer):
        rated = None
        for s in range(unit):
            power = None
            for j in range(3):
                f = 3 * s + j
                field = dot(rows_out[...], buffer[2][f])
                fields[u, f] = field.astype(fields.dtype)
                square = field[:GRID] * field[:GRID] + field[GRID:] * field[GRID:]
                power = square if power is None else power + square
            powers[u, s] = power
            power = value(0, u, s) * power
            rated = power if rated is None else rated + power
        image[...] += rated

    last = units - 1
    mask_fields(0, even)
    columns(even)
    mask_fields(1, odd)

    def forward(u):
        rows(u, even)
        columns(odd)
        mask_fields(u + 2, even)
        rows(u + 1, odd)
        columns(even)
        mask_fields(u + 3, odd)

    def forward_pair(i, carry):
        forward(2 * i)
        return carry

    lax.fori_loop(0, units // 2 - 1, forward_pair, 0)
    rows(last - 1, even)
    columns(odd)
    rows(last, odd)

    total = image[...] * (1.0 / (groups * each * K * K))
    image_out[...] = total

    high, low = halves(total)
    rho = dot(gram[0], high) + dot(gram[0], low) + dot(gram[1], high) - wanted[...]
    double = jnp.concatenate([rho, rho], 0).astype(fields.dtype)

    grad_out[K:] = jnp.zeros_like(grad_out[K:])
    wide[...] = jnp.zeros_like(wide)

    def rows_adjoint(u, buffer):
        for f in range(0, count, 2):
            pair = [fields[u, n] * double for n in (f, f + 1)]
            down = dot(rows_back[...], jnp.concatenate(pair, 1).astype(BF16)).astype(BF16)
            for n in (0, 1):
                one = down[:, n * GRID : (n + 1) * GRID]
                buffer[0][(f + n) * K : (f + n + 1) * K] = one[:K]
                buffer[1][(f + n) * K : (f + n + 1) * K] = one[K:]

    def columns_adjoint(u, buffer):
        both = jnp.concatenate([buffer[0][...], buffer[1][...]], 1)
        back = dot(both, cols_back[...])
        plain_sum = None
        cross_sum = None
        for s in range(unit):
            one = None
            two = None
            for j in range(3):
                f = 3 * s + j
                pupil = pupils[u, f]
                part = back[f * K : (f + 1) * K]
                plain = pupil * part[:, :GRID]
                cross = pupil * part[:, GRID:]
                one = plain if one is None else one + plain
                two = cross if two is None else two + cross
            one = value(0, u, s) * one
            two = value(0, u, s) * two
            plain_sum = one if plain_sum is None else plain_sum + one
            cross_sum = two if cross_sum is None else cross_sum + two
        wide[:, :GRID] += plain_sum
        wide[:, GRID:] += cross_sum

    rows_adjoint(0, even)

    def backward(u):
        columns_adjoint(u, even)
        rows_adjoint(u + 1, odd)
        columns_adjoint(u + 1, odd)
        rows_adjoint(u + 2, even)

    def backward_pair(i, carry):
        backward(2 * i)
        return carry

    lax.fori_loop(0, units // 2 - 1, backward_pair, 0)
    columns_adjoint(last - 1, even)
    rows_adjoint(last, odd)
    columns_adjoint(last, odd)

    scale = norm * 2.0 / (groups * each * K * K)
    one = wide[:, :GRID] * scale
    two = wide[:, GRID:] * scale
    real = one + pltpu.roll(one, K, 1)
    imag = two - pltpu.roll(two, K, 1)
    grad_out[:K] = jnp.where(left, real, -imag)
    terms = jnp.zeros((1, GRID), F32)
    for s in range(each):
        power = powers[s // unit, s % unit]
        term = jnp.sum(jnp.sum(rho * power, 0, keepdims=True), 1, keepdims=True)
        terms = jnp.where(lanes((1, GRID)) == s, term * (1.0 / (K * K)), terms)
    grad_out[K : K + 1] = terms


def own(table, start, share):
    return table[pl.ds(pl.multiple_of(start, share), share), :]


def image_kernel(image, lift_rows, lift_cols, out):
    share = out.shape[1]
    rows = dot_wide(own(lift_rows, lax.axis_index("src") * share, share), image[...])
    out[0] = wide_dot(rows, lift_cols[...])


def mask_kernel(mine, theirs, core_t, rim_t, col_fwd_t, out, source_out, *, pixels):
    each = source_out.shape[1]
    share = out.shape[1]
    left = lanes((K, GRID)) < K
    start = lax.axis_index("src") * share
    rows = 0.0
    for ref, table, first in (
        (mine, core_t, start),
        (theirs, rim_t, lax.axis_index("tile") * core_t.shape[0] + start),
    ):
        top = ref[:K]
        turned = pltpu.roll(top, K, 1)
        both = jnp.concatenate([top, jnp.where(left, -turned, turned)], 0)
        rows += dot_wide(own(table, first, share), both)
    out[0] = GRAD_SCALE * wide_dot(rows, col_fwd_t[...])
    terms = mine[K : K + 1] + theirs[K : K + 1]
    source_out[...] = terms[:, :each] * (1.0 / pixels)


def pack_kernel(weight_far, offset_far, state_far, out, weight, offset, state, sems):
    pairs = [(weight_far, weight), (offset_far, offset), (state_far, state)]
    for copy in fetch(pairs, sems):
        copy.wait()
    out[0:1] = weight[...]
    out[1:3] = offset[...].astype(F32)
    out[3:4] = state[...].astype(F32)


FAR = pl.BlockSpec(memory_space=pltpu.HBM)
VM = pl.BlockSpec(memory_space=pltpu.VMEM)
SM = pl.BlockSpec(memory_space=pltpu.SMEM)


def run(kernel, out_shape, scalars, arrays, flops, scratch=(), held=0, far=False):
    outs = out_shape if isinstance(out_shape, tuple) else (out_shape,)
    if far:
        scratch = [pltpu.VMEM(a.shape, a.dtype) for a in arrays]
        scratch.append(pltpu.SemaphoreType.DMA((len(arrays),)))
        arrays = [pltpu.with_memory_space_constraint(a, pltpu.HBM) for a in arrays]
    size = held + sum(a.size * a.dtype.itemsize for a in (*arrays, *outs))
    return pl.pallas_call(
        kernel,
        out_shape=out_shape,
        in_specs=[SM] * len(scalars) + [FAR if far else VM] * len(arrays),
        out_specs=jax.tree.map(lambda _: VM, out_shape),
        scratch_shapes=scratch,
        compiler_params=pltpu.CompilerParams(vmem_limit_bytes=size + (4 << 20)),
        cost_estimate=pl.CostEstimate(flops=flops, bytes_accessed=size, transcendentals=0),
    )(*scalars, *arrays)


def body(mask_values, target_image, jones_pupil, polar_states, source_weights, pupil_offsets, polar_ids):
    tile_h, tile_w = mask_values.shape
    each = source_weights.shape[0]
    groups = lax.axis_size("src")
    tiles = lax.axis_size("tile")
    share = tile_h // groups
    tab = make_tables(tile_h, tile_w, tiles)
    shape = jax.ShapeDtypeStruct

    known = run(
        pack_kernel, shape((4, each), F32), [],
        [source_weights[None], pupil_offsets.T, polar_ids[None]], flops=1, far=True,
    )
    part, edge = run(
        core_kernel, (shape((tile_h, 2 * K), BF16), shape((AMB, tile_w), BF16)),
        [], [mask_values, tab["col_fwd"]], flops=2**27, far=True,
    )
    halo = flip(edge, "tile", 1)
    wanted = run(
        target_kernel, shape((GRID, GRID), F32), [],
        [target_image, tab["lift_rows_t"], tab["lift_cols_t"]],
        flops=2**27, far=True,
    )
    step = 1
    while step < groups:
        theirs = flip(known, "src", step)
        known = jnp.concatenate([known, theirs], 0)
        step *= 2
    pols = polar_states.shape[0]
    norm = 1.0 / math.sqrt((tile_h + 2 * AMB) * tile_w)
    tables, spectrum = run(
        lambda *refs: prepare_kernel(*refs, norm=norm),
        (shape((6 * pols, GRID, GRID), F32), shape((K, GRID), F32)),
        [polar_states.transpose(1, 2, 0)],
        [jones_pupil.reshape(12, GRID, GRID), part, halo]
        + [tab[n] for n in ("col_fwd", "row_core", "row_halo")],
        flops=48 * pols * GRID * GRID,
    )
    unit = each
    units = groups
    count = 3 * unit
    shapes = [
        ((units, count, K, GRID), F32),
        ((units, count, 2 * GRID, GRID), F32 if groups * each <= 64 else BF16),
        ((units, unit, GRID, GRID), F32),
        ((GRID, GRID), F32),
        ((K, 2 * GRID), F32),
    ]
    shapes += 2 * [
        ((count * K, GRID), BF16),
        ((count * K, GRID), BF16),
        ((count, GRID, GRID), BF16),
    ]
    image, grad = run(
        lambda *refs: source_kernel(*refs, norm=norm),
        (shape((GRID, GRID), F32), shape((K + 8, GRID), F32)),
        [known], [spectrum, wanted, tables]
        + [tab[n] for n in ("cols_out", "rows_out", "rows_back", "cols_back", "gram")],
        flops=2**32,
        scratch=[pltpu.VMEM(*s) for s in shapes],
        held=sum(math.prod(s) * jnp.dtype(d).itemsize for s, d in shapes),
    )
    theirs = flip(grad, "tile", 1)
    own_image = run(
        image_kernel, shape((1, share, tile_w), F32), [],
        [image, tab["lift_rows"], tab["lift_cols"]], flops=2**24,
    )
    own_grad, source_grad = run(
        lambda *refs: mask_kernel(*refs, pixels=tiles * tile_h * tile_w),
        (shape((1, share, tile_w), F32), shape((1, each), F32)), [],
        [grad, theirs, tab["core_t"], tab["rim_t"], tab["col_fwd_t"]], flops=2**24,
    )
    return own_image, own_grad, source_grad.reshape(each)


def solution(mesh):
    placed = (
        P(("parts", "tile"), None),
        P(("parts", "tile"), None),
        P(),
        P(),
        P(("parts", "src")),
        P(("parts", "src"), None),
        P(("parts", "src")),
    )
    return jax.shard_map(
        body,
        mesh=mesh,
        in_specs=placed,
        out_specs=(
            P(("parts", "tile"), "src", None),
            P(("parts", "tile"), "src", None),
            P(("parts", "src")),
        ),
        check_vma=False,
    )
```

```python
import math

import jax
import jax.numpy as jnp
import numpy as np
from jax import lax
from jax.experimental import pallas as pl
from jax.experimental.pallas import tpu as pltpu
from jax.sharding import PartitionSpec as P


AMB = 64
K = 64
GRID = 2 * K
GRAD_SCALE = 32.0
F32 = jnp.float32
BF16 = jnp.bfloat16


def flip(value, axis, mask):
    pairs = [(i, i ^ mask) for i in range(lax.axis_size(axis))]
    return lax.ppermute(value, axis, pairs)


def narrow(table):
    return np.asarray(table, np.float32).astype(jnp.bfloat16)


def split(table):
    high = narrow(table)
    return high, narrow(np.asarray(table, np.float64) - high.astype(np.float64))


def kernel_of_orders(gap):
    orders = np.arange(1, K)
    return (1.0 + 2.0 * np.cos(gap[..., None] * orders).sum(-1)) / GRID


def make_tables(tile_h, tile_w, tiles):
    window = tile_h + 2 * AMB
    two_pi = 2.0 * math.pi
    orders = np.arange(K) - K // 2
    cols = np.arange(tile_w)
    rows = np.arange(window)
    points = np.arange(GRID)
    col = two_pi * np.mod(cols[:, None] * orders[None], tile_w) / tile_w
    row = two_pi * np.mod(orders[:, None] * rows[None], window) / window
    grid = two_pi * np.mod(orders[:, None] * points[None], GRID) / GRID
    cos, sin = np.cos(grid), np.sin(grid)
    col_fwd = np.concatenate([np.cos(col), -np.sin(col)], 1)
    row_fwd = np.concatenate([np.cos(row), np.sin(row)], 0)
    cols_out = np.block([[cos, sin], [-cos, -sin], [-sin, cos], [-sin, cos]])
    rows_out = np.block([[cos.T, -sin.T], [sin.T, cos.T]])
    cols_back = np.block(
        [[cos.T, -sin.T, -sin.T, cos.T], [sin.T, cos.T, cos.T, sin.T]]
    )
    core = np.arange(tile_h) + AMB
    lift_rows = kernel_of_orders(
        two_pi * (core[:, None] / window - points[None] / GRID)
    )
    lift_cols = kernel_of_orders(
        two_pi * (points[:, None] / GRID - cols[None] / tile_w)
    )
    gram = (tile_w / GRID) * lift_rows.T @ lift_rows
    halo = np.stack([row_fwd[:, tile_h + AMB :], row_fwd[:, :AMB]])
    rim = np.zeros((tiles * tile_h, 2 * K))
    rim[tile_h - AMB : tile_h] = row_fwd[:, :AMB].T
    rim[tile_h : tile_h + AMB] = row_fwd[:, tile_h + AMB :].T
    return dict(
        col_fwd=narrow(col_fwd),
        col_fwd_t=narrow(col_fwd.T),
        row_core=narrow(row_fwd[:, AMB : AMB + tile_h]),
        row_halo=narrow(halo),
        cols_out=narrow(cols_out),
        rows_out=narrow(rows_out),
        rows_back=narrow(rows_out.T),
        cols_back=narrow(cols_back),
        lift_rows=narrow(lift_rows),
        lift_rows_t=narrow(lift_rows.T),
        lift_cols=narrow(lift_cols),
        lift_cols_t=narrow(lift_cols.T),
        gram=np.stack(split(gram)),
        core_t=narrow(row_fwd[:, AMB : AMB + tile_h].T),
        rim_t=narrow(rim),
    )


def dot(a, b):
    return jnp.dot(a, b, preferred_element_type=F32)


def halves(value):
    high = value.astype(BF16)
    return high, (value - high.astype(F32)).astype(BF16)


def dot_wide(table, value):
    high, low = halves(value)
    return dot(table, high) + dot(table, low)


def wide_dot(value, table):
    high, low = halves(value)
    return dot(high, table) + dot(low, table)


def lanes(shape):
    return lax.broadcasted_iota(jnp.int32, shape, 1)


def prepare_kernel(
    polar, jones, part, halo, col_fwd, row_core, row_halo, tables, spectrum, *, norm
):
    left = lanes((K, GRID)) < K
    edge = dot(halo[...], col_fwd[...]).astype(BF16)
    whole = dot(row_core[...], part[...]) + dot(row_halo[lax.axis_index("tile")], edge)
    turned = pltpu.roll(whole[K:], K, 1)
    spectrum[...] = norm * (whole[:K] + jnp.where(left, turned, -turned))
    for pol in range(polar.shape[2]):
        ar, br, ai, bi = (polar[n // 2, n % 2, pol] for n in range(4))
        for j in range(3):
            real = jones[2 * j] * ar - jones[6 + 2 * j] * ai
            real += jones[2 * j + 1] * br - jones[6 + 2 * j + 1] * bi
            imag = jones[2 * j] * ai + jones[6 + 2 * j] * ar
            imag += jones[2 * j + 1] * bi + jones[6 + 2 * j + 1] * br
            tables[2 * (3 * pol + j)] = real
            tables[2 * (3 * pol + j) + 1] = pltpu.roll(imag, K, 1)


def fetch(pairs, sems):
    copies = [pltpu.make_async_copy(a, b, sems.at[n]) for n, (a, b) in enumerate(pairs)]
    for copy in copies:
        copy.start()
    return copies


def core_kernel(mask_far, col_far, part, edge, mask, col_fwd, sems):
    copies = fetch([(mask_far, mask), (col_far, col_fwd)], sems)
    for copy in copies:
        copy.wait()
    start = (1 - lax.axis_index("tile")) * (mask.shape[0] - AMB)
    edge[...] = mask[pl.ds(pl.multiple_of(start, AMB), AMB), :]
    part[...] = dot(mask[...], col_fwd[...]).astype(BF16)


def target_kernel(
    target_far, rows_far, cols_far, wanted, target, lift_rows_t, lift_cols_t, sems
):
    pairs = [(target_far, target), (rows_far, lift_rows_t), (cols_far, lift_cols_t)]
    for copy in fetch(pairs, sems):
        copy.wait()
    seen = dot(lift_rows_t[...], target[...].astype(BF16)).astype(BF16)
    wanted[...] = dot(seen, lift_cols_t[...])


def repeat(step, pairs, most):
    each = most if pairs % most == 0 else 1

    def steps(i, carry):
        for n in range(each):
            step(2 * (each * i + n))
        return carry

    if pairs == each:
        steps(0, 0)
    else:
        lax.fori_loop(0, pairs // each, steps, 0)


def source_kernel(
    known, spectrum, wanted, tables,
    cols_out, rows_out, rows_back, cols_back, gram,
    image_out, grad_out,
    pupils, fields, powers, image, wide, *buffers,
    norm,
):
    each = known.shape[1]
    groups = known.shape[0] // 4
    units, count = fields.shape[:2]
    unit = count // 3
    even, odd = buffers[:3], buffers[3:]
    left = lanes((K, GRID)) < K

    first = spectrum[...]
    second = pltpu.roll(first, K, 1)

    image[...] = jnp.zeros_like(image)

    def value(row, u, s):
        n = u * unit + s
        group = lax.div(n, each)
        return known[4 * group + row, n - group * each]

    def mask_fields(u, s, buffer):
        up, side, pol = (value(row, u, s).astype(jnp.int32) for row in (1, 2, 3))
        inside = (lanes((K, GRID)) >= side) & (lanes((K, GRID)) < side + K)
        turn = jnp.where(side == 0, 0, GRID - side)
        for j in range(3):
            real = tables[2 * (3 * pol + j), pl.ds(up, K), :]
            imag = tables[2 * (3 * pol + j) + 1, pl.ds(up, K), :]
            pupil = pltpu.roll(jnp.where(inside, real, imag), turn, 1)
            f = 3 * s + j
            pupils[u, f] = pupil
            buffer[0][f * K : (f + 1) * K] = (pupil * first).astype(BF16)
            buffer[1][f * K : (f + 1) * K] = (pupil * second).astype(BF16)

    def columns(s, buffer):
        part = slice(3 * s * K, 3 * (s + 1) * K)
        both = jnp.concatenate([buffer[0][part], buffer[1][part]], 1)
        across = dot(both, cols_out[...]).astype(BF16)
        for j in range(3):
            part = across[j * K : (j + 1) * K]
            buffer[2][3 * s + j, :K] = part[:, :GRID]
            buffer[2][3 * s + j, K:] = part[:, GRID:]

    def rows(u, s, buffer):
        power = None
        for j in range(3):
            f = 3 * s + j
            field = dot(rows_out[...], buffer[2][f])
            fields[u, f] = field.astype(fields.dtype)
            square = field[:GRID] * field[:GRID] + field[GRID:] * field[GRID:]
            power = square if power is None else power + square
        powers[u, s] = power

    last = units - 1
    for s in range(unit):
        mask_fields(0, s, even)
    for s in range(unit):
        columns(s, even)
        mask_fields(1, s, odd)

    def forward(u):
        for s in range(unit):
            columns(s, odd)
            rows(u, s, even)
            mask_fields(u + 2, s, even)
        for s in range(unit):
            columns(s, even)
            rows(u + 1, s, odd)
            mask_fields(u + 3, s, odd)

    repeat(forward, units // 2 - 1, 3)
    for s in range(unit):
        columns(s, odd)
        rows(last - 1, s, even)
    for s in range(unit):
        rows(last, s, odd)

    def gather(u, carry):
        rated = value(0, u, 0) * powers[u, 0]
        for s in range(1, unit):
            rated += value(0, u, s) * powers[u, s]
        image[...] += rated
        return carry

    lax.fori_loop(0, units, gather, 0)
    total = image[...] * (1.0 / (groups * each * K * K))
    image_out[...] = total

    high, low = halves(total)
    rho = dot(gram[0], high) + dot(gram[0], low) + dot(gram[1], high) - wanted[...]
    double = jnp.concatenate([rho, rho], 0).astype(fields.dtype)

    grad_out[K:] = jnp.zeros_like(grad_out[K:])
    wide[...] = jnp.zeros_like(wide)

    def rows_adjoint(u, h, buffer):
        for f in range(6 * h, 6 * h + 6, 2):
            pair = [fields[u, n] * double for n in (f, f + 1)]
            down = dot(rows_back[...], jnp.concatenate(pair, 1).astype(BF16)).astype(BF16)
            for n in (0, 1):
                one = down[:, n * GRID : (n + 1) * GRID]
                buffer[0][(f + n) * K : (f + n + 1) * K] = one[:K]
                buffer[1][(f + n) * K : (f + n + 1) * K] = one[K:]

    def columns_adjoint(u, h, buffer):
        part = slice(6 * h * K, 6 * (h + 1) * K)
        both = jnp.concatenate([buffer[0][part], buffer[1][part]], 1)
        back = dot(both, cols_back[...])
        for s in (2 * h, 2 * h + 1):
            one = None
            two = None
            for j in range(3):
                f = 3 * s + j - 6 * h
                pupil = pupils[u, 3 * s + j]
                part = back[f * K : (f + 1) * K]
                plain = pupil * part[:, :GRID]
                cross = pupil * part[:, GRID:]
                one = plain if one is None else one + plain
                two = cross if two is None else two + cross
            wide[:, :GRID] += value(0, u, s) * one
            wide[:, GRID:] += value(0, u, s) * two

    two_each = range(unit // 2)
    for h in two_each:
        rows_adjoint(0, h, even)

    def backward(u):
        for h in two_each:
            columns_adjoint(u, h, even)
            rows_adjoint(u + 1, h, odd)
        for h in two_each:
            columns_adjoint(u + 1, h, odd)
            rows_adjoint(u + 2, h, even)

    repeat(backward, units // 2 - 1, 3)
    for h in two_each:
        columns_adjoint(last - 1, h, even)
        rows_adjoint(last, h, odd)
    for h in two_each:
        columns_adjoint(last, h, odd)

    scale = norm * 2.0 / (groups * each * K * K)
    one = wide[:, :GRID] * scale
    two = wide[:, GRID:] * scale
    real = one + pltpu.roll(one, K, 1)
    imag = two - pltpu.roll(two, K, 1)
    grad_out[:K] = jnp.where(left, real, -imag)
    terms = jnp.zeros((1, GRID), F32)
    for s in range(each):
        power = powers[s // unit, s % unit]
        term = jnp.sum(jnp.sum(rho * power, 0, keepdims=True), 1, keepdims=True)
        terms = jnp.where(lanes((1, GRID)) == s, term * (1.0 / (K * K)), terms)
    grad_out[K : K + 1] = terms


def own(table, start, share):
    return table[pl.ds(pl.multiple_of(start, share), share), :]


def image_kernel(image, lift_rows, lift_cols, out):
    share = out.shape[1]
    rows = dot_wide(own(lift_rows, lax.axis_index("src") * share, share), image[...])
    out[0] = wide_dot(rows, lift_cols[...])


def mask_kernel(mine, theirs, core_t, rim_t, col_fwd_t, out, source_out, *, pixels):
    each = source_out.shape[1]
    share = out.shape[1]
    left = lanes((K, GRID)) < K
    start = lax.axis_index("src") * share
    rows = 0.0
    for ref, table, first in (
        (mine, core_t, start),
        (theirs, rim_t, lax.axis_index("tile") * core_t.shape[0] + start),
    ):
        top = ref[:K]
        turned = pltpu.roll(top, K, 1)
        both = jnp.concatenate([top, jnp.where(left, -turned, turned)], 0)
        rows += dot_wide(own(table, first, share), both)
    out[0] = GRAD_SCALE * wide_dot(rows, col_fwd_t[...])
    terms = mine[K : K + 1] + theirs[K : K + 1]
    source_out[...] = terms[:, :each] * (1.0 / pixels)


def pack_kernel(weight_far, offset_far, state_far, out, weight, offset, state, sems):
    pairs = [(weight_far, weight), (offset_far, offset), (state_far, state)]
    for copy in fetch(pairs, sems):
        copy.wait()
    out[0:1] = weight[...]
    out[1:3] = offset[...].astype(F32)
    out[3:4] = state[...].astype(F32)


FAR = pl.BlockSpec(memory_space=pltpu.HBM)
VM = pl.BlockSpec(memory_space=pltpu.VMEM)
SM = pl.BlockSpec(memory_space=pltpu.SMEM)


def run(kernel, out_shape, scalars, arrays, flops, scratch=(), held=0, far=False):
    outs = out_shape if isinstance(out_shape, tuple) else (out_shape,)
    if far:
        scratch = [pltpu.VMEM(a.shape, a.dtype) for a in arrays]
        scratch.append(pltpu.SemaphoreType.DMA((len(arrays),)))
        arrays = [pltpu.with_memory_space_constraint(a, pltpu.HBM) for a in arrays]
    size = held + sum(a.size * a.dtype.itemsize for a in (*arrays, *outs))
    return pl.pallas_call(
        kernel,
        out_shape=out_shape,
        in_specs=[SM] * len(scalars) + [FAR if far else VM] * len(arrays),
        out_specs=jax.tree.map(lambda _: VM, out_shape),
        scratch_shapes=scratch,
        compiler_params=pltpu.CompilerParams(vmem_limit_bytes=size + (4 << 20)),
        cost_estimate=pl.CostEstimate(flops=flops, bytes_accessed=size, transcendentals=0),
    )(*scalars, *arrays)


def body(mask_values, target_image, jones_pupil, polar_states, source_weights, pupil_offsets, polar_ids):
    tile_h, tile_w = mask_values.shape
    each = source_weights.shape[0]
    groups = lax.axis_size("src")
    tiles = lax.axis_size("tile")
    share = tile_h // groups
    tab = make_tables(tile_h, tile_w, tiles)
    shape = jax.ShapeDtypeStruct

    known = run(
        pack_kernel, shape((4, each), F32), [],
        [source_weights[None], pupil_offsets.T, polar_ids[None]], flops=1, far=True,
    )
    part, edge = run(
        core_kernel, (shape((tile_h, 2 * K), BF16), shape((AMB, tile_w), BF16)),
        [], [mask_values, tab["col_fwd"]], flops=2**27, far=True,
    )
    halo = flip(edge, "tile", 1)
    wanted = run(
        target_kernel, shape((GRID, GRID), F32), [],
        [target_image, tab["lift_rows_t"], tab["lift_cols_t"]],
        flops=2**27, far=True,
    )
    step = 1
    while step < groups:
        theirs = flip(known, "src", step)
        known = jnp.concatenate([known, theirs], 0)
        step *= 2
    pols = polar_states.shape[0]
    norm = 1.0 / math.sqrt((tile_h + 2 * AMB) * tile_w)
    tables, spectrum = run(
        lambda *refs: prepare_kernel(*refs, norm=norm),
        (shape((6 * pols, GRID, GRID), F32), shape((K, GRID), F32)),
        [polar_states.transpose(1, 2, 0)],
        [jones_pupil.reshape(12, GRID, GRID), part, halo]
        + [tab[n] for n in ("col_fwd", "row_core", "row_halo")],
        flops=48 * pols * GRID * GRID,
    )
    unit = each
    units = groups
    count = 3 * unit
    shapes = [
        ((units, count, K, GRID), F32),
        ((units, count, 2 * GRID, GRID), F32 if groups * each <= 64 else BF16),
        ((units, unit, GRID, GRID), F32),
        ((GRID, GRID), F32),
        ((K, 2 * GRID), F32),
    ]
    shapes += 2 * [
        ((count * K, GRID), BF16),
        ((count * K, GRID), BF16),
        ((count, GRID, GRID), BF16),
    ]
    image, grad = run(
        lambda *refs: source_kernel(*refs, norm=norm),
        (shape((GRID, GRID), F32), shape((K + 8, GRID), F32)),
        [known], [spectrum, wanted, tables]
        + [tab[n] for n in ("cols_out", "rows_out", "rows_back", "cols_back", "gram")],
        flops=2**32,
        scratch=[pltpu.VMEM(*s) for s in shapes],
        held=sum(math.prod(s) * jnp.dtype(d).itemsize for s, d in shapes),
    )
    theirs = flip(grad, "tile", 1)
    own_image = run(
        image_kernel, shape((1, share, tile_w), F32), [],
        [image, tab["lift_rows"], tab["lift_cols"]], flops=2**24,
    )
    own_grad, source_grad = run(
        lambda *refs: mask_kernel(*refs, pixels=tiles * tile_h * tile_w),
        (shape((1, share, tile_w), F32), shape((1, each), F32)), [],
        [grad, theirs, tab["core_t"], tab["rim_t"], tab["col_fwd_t"]], flops=2**24,
    )
    return own_image, own_grad, source_grad.reshape(each)


def solution(mesh):
    placed = (
        P(("parts", "tile"), None),
        P(("parts", "tile"), None),
        P(),
        P(),
        P(("parts", "src")),
        P(("parts", "src"), None),
        P(("parts", "src")),
    )
    return jax.shard_map(
        body,
        mesh=mesh,
        in_specs=placed,
        out_specs=(
            P(("parts", "tile"), "src", None),
            P(("parts", "tile"), "src", None),
            P(("parts", "src")),
        ),
        check_vma=False,
    )
```

```python
import math

import jax
import jax.numpy as jnp
import numpy as np
from jax import lax
from jax.experimental import pallas as pl
from jax.experimental.pallas import tpu as pltpu
from jax.sharding import PartitionSpec as P


AMB = 64
K = 64
GRID = 2 * K
GRAD_SCALE = 32.0
F32 = jnp.float32
BF16 = jnp.bfloat16


def flip(value, axis, mask):
    pairs = [(i, i ^ mask) for i in range(lax.axis_size(axis))]
    return lax.ppermute(value, axis, pairs)


def narrow(table):
    return np.asarray(table, np.float32).astype(jnp.bfloat16)


def split(table):
    high = narrow(table)
    return high, narrow(np.asarray(table, np.float64) - high.astype(np.float64))


def kernel_of_orders(gap):
    orders = np.arange(1, K)
    return (1.0 + 2.0 * np.cos(gap[..., None] * orders).sum(-1)) / GRID


def make_tables(tile_h, tile_w, tiles):
    window = tile_h + 2 * AMB
    two_pi = 2.0 * math.pi
    orders = np.arange(K) - K // 2
    cols = np.arange(tile_w)
    rows = np.arange(window)
    points = np.arange(GRID)
    col = two_pi * np.mod(cols[:, None] * orders[None], tile_w) / tile_w
    row = two_pi * np.mod(orders[:, None] * rows[None], window) / window
    grid = two_pi * np.mod(orders[:, None] * points[None], GRID) / GRID
    cos, sin = np.cos(grid), np.sin(grid)
    col_fwd = np.concatenate([np.cos(col), -np.sin(col)], 1)
    row_fwd = np.concatenate([np.cos(row), np.sin(row)], 0)
    cols_out = np.block([[cos, sin], [-cos, -sin], [-sin, cos], [-sin, cos]])
    rows_out = np.block([[cos.T, -sin.T], [sin.T, cos.T]])
    cols_back = np.block(
        [[cos.T, -sin.T, -sin.T, cos.T], [sin.T, cos.T, cos.T, sin.T]]
    )
    core = np.arange(tile_h) + AMB
    lift_rows = kernel_of_orders(
        two_pi * (core[:, None] / window - points[None] / GRID)
    )
    lift_cols = kernel_of_orders(
        two_pi * (points[:, None] / GRID - cols[None] / tile_w)
    )
    gram = (tile_w / GRID) * lift_rows.T @ lift_rows
    halo = np.stack([row_fwd[:, tile_h + AMB :], row_fwd[:, :AMB]])
    rim = np.zeros((tiles * tile_h, 2 * K))
    rim[tile_h - AMB : tile_h] = row_fwd[:, :AMB].T
    rim[tile_h : tile_h + AMB] = row_fwd[:, tile_h + AMB :].T
    return dict(
        col_fwd=narrow(col_fwd),
        col_fwd_t=narrow(col_fwd.T),
        row_core=narrow(row_fwd[:, AMB : AMB + tile_h]),
        row_halo=narrow(halo),
        cols_out=narrow(cols_out),
        rows_out=narrow(rows_out),
        rows_back=narrow(rows_out.T),
        cols_back=narrow(cols_back),
        lift_rows=narrow(lift_rows),
        lift_rows_t=narrow(lift_rows.T),
        lift_cols=narrow(lift_cols),
        lift_cols_t=narrow(lift_cols.T),
        gram=np.stack(split(gram)),
        core_t=narrow(row_fwd[:, AMB : AMB + tile_h].T),
        rim_t=narrow(rim),
    )


def dot(a, b):
    return jnp.dot(a, b, preferred_element_type=F32)


def halves(value):
    high = value.astype(BF16)
    return high, (value - high.astype(F32)).astype(BF16)


def dot_wide(table, value):
    high, low = halves(value)
    return dot(table, high) + dot(table, low)


def wide_dot(value, table):
    high, low = halves(value)
    return dot(high, table) + dot(low, table)


def lanes(shape):
    return lax.broadcasted_iota(jnp.int32, shape, 1)


def prepare_kernel(
    polar, jones, part, halo, col_fwd, row_core, row_halo, tables, spectrum, *, norm
):
    left = lanes((K, GRID)) < K
    edge = dot(halo[...], col_fwd[...]).astype(BF16)
    whole = dot(row_core[...], part[...]) + dot(row_halo[lax.axis_index("tile")], edge)
    turned = pltpu.roll(whole[K:], K, 1)
    spectrum[...] = norm * (whole[:K] + jnp.where(left, turned, -turned))
    for pol in range(polar.shape[2]):
        ar, br, ai, bi = (polar[n // 2, n % 2, pol] for n in range(4))
        for j in range(3):
            real = jones[2 * j] * ar - jones[6 + 2 * j] * ai
            real += jones[2 * j + 1] * br - jones[6 + 2 * j + 1] * bi
            imag = jones[2 * j] * ai + jones[6 + 2 * j] * ar
            imag += jones[2 * j + 1] * bi + jones[6 + 2 * j + 1] * br
            tables[2 * (3 * pol + j)] = real
            tables[2 * (3 * pol + j) + 1] = pltpu.roll(imag, K, 1)


def fetch(pairs, sems):
    copies = [pltpu.make_async_copy(a, b, sems.at[n]) for n, (a, b) in enumerate(pairs)]
    for copy in copies:
        copy.start()
    return copies


def core_kernel(mask_far, col_far, part, edge, mask, col_fwd, sems):
    copies = fetch([(mask_far, mask), (col_far, col_fwd)], sems)
    for copy in copies:
        copy.wait()
    start = (1 - lax.axis_index("tile")) * (mask.shape[0] - AMB)
    edge[...] = mask[pl.ds(pl.multiple_of(start, AMB), AMB), :]
    part[...] = dot(mask[...], col_fwd[...]).astype(BF16)


def target_kernel(
    target_far, rows_far, cols_far, wanted, target, lift_rows_t, lift_cols_t, sems
):
    pairs = [(target_far, target), (rows_far, lift_rows_t), (cols_far, lift_cols_t)]
    for copy in fetch(pairs, sems):
        copy.wait()
    seen = dot(lift_rows_t[...], target[...].astype(BF16)).astype(BF16)
    wanted[...] = dot(seen, lift_cols_t[...])


def repeat(step, pairs, most):
    each = most if pairs % most == 0 else 1

    def steps(i, carry):
        for n in range(each):
            step(2 * (each * i + n))
        return carry

    if pairs == each:
        steps(0, 0)
    else:
        lax.fori_loop(0, pairs // each, steps, 0)


def source_kernel(
    known, spectrum, wanted, tables,
    cols_out, rows_out, rows_back, cols_back, gram,
    image_out, grad_out,
    pupils, fields, powers, wide, *buffers,
    norm,
):
    each = known.shape[1]
    groups = known.shape[0] // 4
    units, count = fields.shape[:2]
    unit = count // 3
    even, odd = buffers[:3], buffers[3:]
    left = lanes((K, GRID)) < K

    first = spectrum[...]
    second = pltpu.roll(first, K, 1)

    def value(row, u, s):
        n = u * unit + s
        group = lax.div(n, each)
        return known[4 * group + row, n - group * each]

    def mask_fields(u, s, buffer):
        up, side, pol = (value(row, u, s).astype(jnp.int32) for row in (1, 2, 3))
        inside = (lanes((K, GRID)) >= side) & (lanes((K, GRID)) < side + K)
        turn = jnp.where(side == 0, 0, GRID - side)
        for j in range(3):
            real = tables[2 * (3 * pol + j), pl.ds(up, K), :]
            imag = tables[2 * (3 * pol + j) + 1, pl.ds(up, K), :]
            pupil = pltpu.roll(jnp.where(inside, real, imag), turn, 1)
            f = 3 * s + j
            pupils[u, f] = pupil
            buffer[0][f * K : (f + 1) * K] = (pupil * first).astype(BF16)
            buffer[1][f * K : (f + 1) * K] = (pupil * second).astype(BF16)

    def columns(s, buffer):
        part = slice(3 * s * K, 3 * (s + 1) * K)
        both = jnp.concatenate([buffer[0][part], buffer[1][part]], 1)
        across = dot(both, cols_out[...]).astype(BF16)
        for j in range(3):
            part = across[j * K : (j + 1) * K]
            buffer[2][3 * s + j, :K] = part[:, :GRID]
            buffer[2][3 * s + j, K:] = part[:, GRID:]

    def rows(u, s, buffer):
        power = None
        for j in range(3):
            f = 3 * s + j
            field = dot(rows_out[...], buffer[2][f])
            fields[u, f] = field.astype(fields.dtype)
            square = field[:GRID] * field[:GRID] + field[GRID:] * field[GRID:]
            power = square if power is None else power + square
        powers[u, s] = power

    last = units - 1
    for s in range(unit):
        mask_fields(0, s, even)
    for s in range(unit):
        columns(s, even)
        mask_fields(1, s, odd)

    def forward(u):
        for s in range(unit):
            columns(s, odd)
            rows(u, s, even)
            mask_fields(u + 2, s, even)
        for s in range(unit):
            columns(s, even)
            rows(u + 1, s, odd)
            mask_fields(u + 3, s, odd)

    repeat(forward, units // 2 - 1, 3)
    for s in range(unit):
        columns(s, odd)
        rows(last - 1, s, even)
    for s in range(unit):
        rows(last, s, odd)

    def gather(i, rated):
        for n in range(2):
            u = 2 * i + n
            for s in range(unit):
                rated += value(0, u, s) * powers[u, s]
        return rated

    rated = lax.fori_loop(0, units // 2, gather, jnp.zeros((GRID, GRID), F32))
    total = rated * (1.0 / (groups * each * K * K))
    image_out[...] = total

    high, low = halves(total)
    rho = dot(gram[0], high) + dot(gram[0], low) + dot(gram[1], high) - wanted[...]
    double = jnp.concatenate([rho, rho], 0).astype(fields.dtype)

    grad_out[K:] = jnp.zeros_like(grad_out[K:])
    wide[...] = jnp.zeros_like(wide)

    def rows_adjoint(u, h, buffer):
        for f in range(6 * h, 6 * h + 6, 2):
            pair = [fields[u, n] * double for n in (f, f + 1)]
            down = dot(rows_back[...], jnp.concatenate(pair, 1).astype(BF16)).astype(BF16)
            for n in (0, 1):
                one = down[:, n * GRID : (n + 1) * GRID]
                buffer[0][(f + n) * K : (f + n + 1) * K] = one[:K]
                buffer[1][(f + n) * K : (f + n + 1) * K] = one[K:]

    def columns_adjoint(u, h, buffer):
        part = slice(6 * h * K, 6 * (h + 1) * K)
        both = jnp.concatenate([buffer[0][part], buffer[1][part]], 1)
        back = dot(both, cols_back[...])
        for s in (2 * h, 2 * h + 1):
            one = None
            two = None
            for j in range(3):
                f = 3 * s + j - 6 * h
                pupil = pupils[u, 3 * s + j]
                part = back[f * K : (f + 1) * K]
                plain = pupil * part[:, :GRID]
                cross = pupil * part[:, GRID:]
                one = plain if one is None else one + plain
                two = cross if two is None else two + cross
            wide[:, :GRID] += value(0, u, s) * one
            wide[:, GRID:] += value(0, u, s) * two

    two_each = range(unit // 2)
    for h in two_each:
        rows_adjoint(0, h, even)

    def backward(u):
        for h in two_each:
            columns_adjoint(u, h, even)
            rows_adjoint(u + 1, h, odd)
        for h in two_each:
            columns_adjoint(u + 1, h, odd)
            rows_adjoint(u + 2, h, even)

    repeat(backward, units // 2 - 1, 3)
    for h in two_each:
        columns_adjoint(last - 1, h, even)
        rows_adjoint(last, h, odd)
    for h in two_each:
        columns_adjoint(last, h, odd)

    scale = norm * 2.0 / (groups * each * K * K)
    one = wide[:, :GRID] * scale
    two = wide[:, GRID:] * scale
    real = one + pltpu.roll(one, K, 1)
    imag = two - pltpu.roll(two, K, 1)
    grad_out[:K] = jnp.where(left, real, -imag)
    terms = jnp.zeros((1, GRID), F32)
    for s in range(each):
        power = powers[s // unit, s % unit]
        term = jnp.sum(jnp.sum(rho * power, 0, keepdims=True), 1, keepdims=True)
        terms = jnp.where(lanes((1, GRID)) == s, term * (1.0 / (K * K)), terms)
    grad_out[K : K + 1] = terms


def own(table, start, share):
    return table[pl.ds(pl.multiple_of(start, share), share), :]


def image_kernel(image, lift_rows, lift_cols, out):
    share = out.shape[1]
    rows = dot_wide(own(lift_rows, lax.axis_index("src") * share, share), image[...])
    out[0] = wide_dot(rows, lift_cols[...])


def mask_kernel(mine, theirs, core_t, rim_t, col_fwd_t, out, source_out, *, pixels):
    each = source_out.shape[1]
    share = out.shape[1]
    left = lanes((K, GRID)) < K
    start = lax.axis_index("src") * share
    rows = 0.0
    for ref, table, first in (
        (mine, core_t, start),
        (theirs, rim_t, lax.axis_index("tile") * core_t.shape[0] + start),
    ):
        top = ref[:K]
        turned = pltpu.roll(top, K, 1)
        both = jnp.concatenate([top, jnp.where(left, -turned, turned)], 0)
        rows += dot_wide(own(table, first, share), both)
    out[0] = GRAD_SCALE * wide_dot(rows, col_fwd_t[...])
    terms = mine[K : K + 1] + theirs[K : K + 1]
    source_out[...] = terms[:, :each] * (1.0 / pixels)


def pack_kernel(weight_far, offset_far, state_far, out, weight, offset, state, sems):
    pairs = [(weight_far, weight), (offset_far, offset), (state_far, state)]
    for copy in fetch(pairs, sems):
        copy.wait()
    out[0:1] = weight[...]
    out[1:3] = offset[...].astype(F32)
    out[3:4] = state[...].astype(F32)


FAR = pl.BlockSpec(memory_space=pltpu.HBM)
VM = pl.BlockSpec(memory_space=pltpu.VMEM)
SM = pl.BlockSpec(memory_space=pltpu.SMEM)


def run(kernel, out_shape, scalars, arrays, flops, scratch=(), held=0, far=False):
    outs = out_shape if isinstance(out_shape, tuple) else (out_shape,)
    if far:
        scratch = [pltpu.VMEM(a.shape, a.dtype) for a in arrays]
        scratch.append(pltpu.SemaphoreType.DMA((len(arrays),)))
        arrays = [pltpu.with_memory_space_constraint(a, pltpu.HBM) for a in arrays]
    size = held + sum(a.size * a.dtype.itemsize for a in (*arrays, *outs))
    return pl.pallas_call(
        kernel,
        out_shape=out_shape,
        in_specs=[SM] * len(scalars) + [FAR if far else VM] * len(arrays),
        out_specs=jax.tree.map(lambda _: VM, out_shape),
        scratch_shapes=scratch,
        compiler_params=pltpu.CompilerParams(vmem_limit_bytes=size + (4 << 20)),
        cost_estimate=pl.CostEstimate(flops=flops, bytes_accessed=size, transcendentals=0),
    )(*scalars, *arrays)


def body(mask_values, target_image, jones_pupil, polar_states, source_weights, pupil_offsets, polar_ids):
    tile_h, tile_w = mask_values.shape
    each = source_weights.shape[0]
    groups = lax.axis_size("src")
    tiles = lax.axis_size("tile")
    share = tile_h // groups
    tab = make_tables(tile_h, tile_w, tiles)
    shape = jax.ShapeDtypeStruct

    known = run(
        pack_kernel, shape((4, each), F32), [],
        [source_weights[None], pupil_offsets.T, polar_ids[None]], flops=1, far=True,
    )
    part, edge = run(
        core_kernel, (shape((tile_h, 2 * K), BF16), shape((AMB, tile_w), BF16)),
        [], [mask_values, tab["col_fwd"]], flops=2**27, far=True,
    )
    halo = flip(edge, "tile", 1)
    wanted = run(
        target_kernel, shape((GRID, GRID), F32), [],
        [target_image, tab["lift_rows_t"], tab["lift_cols_t"]],
        flops=2**27, far=True,
    )
    step = 1
    while step < groups:
        theirs = flip(known, "src", step)
        known = jnp.concatenate([known, theirs], 0)
        step *= 2
    pols = polar_states.shape[0]
    norm = 1.0 / math.sqrt((tile_h + 2 * AMB) * tile_w)
    tables, spectrum = run(
        lambda *refs: prepare_kernel(*refs, norm=norm),
        (shape((6 * pols, GRID, GRID), F32), shape((K, GRID), F32)),
        [polar_states.transpose(1, 2, 0)],
        [jones_pupil.reshape(12, GRID, GRID), part, halo]
        + [tab[n] for n in ("col_fwd", "row_core", "row_halo")],
        flops=48 * pols * GRID * GRID,
    )
    unit = each
    units = groups
    count = 3 * unit
    shapes = [
        ((units, count, K, GRID), F32),
        ((units, count, 2 * GRID, GRID), F32 if groups * each <= 64 else BF16),
        ((units, unit, GRID, GRID), F32),
        ((K, 2 * GRID), F32),
    ]
    shapes += 2 * [
        ((count * K, GRID), BF16),
        ((count * K, GRID), BF16),
        ((count, GRID, GRID), BF16),
    ]
    image, grad = run(
        lambda *refs: source_kernel(*refs, norm=norm),
        (shape((GRID, GRID), F32), shape((K + 8, GRID), F32)),
        [known], [spectrum, wanted, tables]
        + [tab[n] for n in ("cols_out", "rows_out", "rows_back", "cols_back", "gram")],
        flops=2**32,
        scratch=[pltpu.VMEM(*s) for s in shapes],
        held=sum(math.prod(s) * jnp.dtype(d).itemsize for s, d in shapes),
    )
    theirs = flip(grad, "tile", 1)
    own_image = run(
        image_kernel, shape((1, share, tile_w), F32), [],
        [image, tab["lift_rows"], tab["lift_cols"]], flops=2**24,
    )
    own_grad, source_grad = run(
        lambda *refs: mask_kernel(*refs, pixels=tiles * tile_h * tile_w),
        (shape((1, share, tile_w), F32), shape((1, each), F32)), [],
        [grad, theirs, tab["core_t"], tab["rim_t"], tab["col_fwd_t"]], flops=2**24,
    )
    return own_image, own_grad, source_grad.reshape(each)


def solution(mesh):
    placed = (
        P(("parts", "tile"), None),
        P(("parts", "tile"), None),
        P(),
        P(),
        P(("parts", "src")),
        P(("parts", "src"), None),
        P(("parts", "src")),
    )
    return jax.shard_map(
        body,
        mesh=mesh,
        in_specs=placed,
        out_specs=(
            P(("parts", "tile"), "src", None),
            P(("parts", "tile"), "src", None),
            P(("parts", "src")),
        ),
        check_vma=False,
    )
```
